128 devices in a mesh: stn: 16 (over x_hi, z, core), freq: 8 (over x_lo, y).
Axes of the slice: x: 4 (x_hi: 2, x_lo: 2; x = x_hi * 2 + x_lo), y: 4, z: 4, core: 2. Of those that a mesh axis runs over, the one named last changes fastest.
Arguments:
- propagator: bfloat16 [48, 2000, 2000], P('stn'), may hold values from -0.125 to 0.125
- forcing: bfloat16 [48, 2, 512, 2000], P('stn', None, 'freq'), may hold values from -6 to 6
- forward: bfloat16 [48, 2, 512, 2000], P('stn', None, 'freq'), may hold values from -6 to 6
- damping: float32 [2000], replicated, may hold values from 0.0005 to 0.05
- slowness: float32 [2000], replicated, may hold values from 0.5 to 2
- station_gap: int32 [48], P('stn'), may hold values from 1 to 3
- freq_index: int32 [512], P('freq'), may hold values from 0 to 511, each once
Outputs:
- sensitivity: float32 [48, 2000], P('stn', 'freq')
The draws below stay inside these ranges and needn't reach their ends.
Inputs may be any that keep to these rules, and one draw needn't show every extreme that they name: `freq_index`: each index of the list appears exactly once.
All inputs are finite; a program needn't handle non-finite values.
Results may differ from the reference program's by a relative error of at most 0.018.
Values may be sent and summed in bfloat16 or wider, within the bound.
No kernel may reach another device: no remote copies, remote signals or barrier semaphores. Data moves between devices by JAX's collectives and lax.ppermute only.
A program may use at most 128 MiB of HBM per device.

```python
import math
import jax
import jax.numpy as jnp
from jax import lax

NVAR = 5
NWALL = 400
M = 2000
NSTN = 48
NFREQ = 512


def with_ends(entries, stream_key, least, largest):
    longest = entries.shape.index(max(entries.shape))
    spots = []
    for shift in (0, 1):
        where = [jax.random.randint(jax.random.fold_in(stream_key, axis), (), 0, length) for axis, length in enumerate(entries.shape)]
        where[longest] = (where[longest] + shift) % entries.shape[longest]
        spots.append(tuple(where))
    return entries.at[spots[0]].set(least).at[spots[1]].set(largest)


def block_levels(stream_key, dims, cuts, smallest, top_value):
    def one(position, parts):
        heights = jax.random.uniform(jax.random.fold_in(jax.random.fold_in(stream_key, 6), position), (parts,), jnp.float32, smallest / len(cuts), top_value / len(cuts))
        return jnp.repeat(jnp.exp(heights), dims[position] // parts).reshape((-1,) + (1,) * (len(dims) - position - 1))

    level = one(*cuts[0])
    for cut in cuts[1:]:
        level = level * one(*cut)
    return level


def scatter_about(rng, shape, spread, limit, cuts=(), kind=jnp.bfloat16):
    array = jax.random.normal(rng, shape, jnp.float32) * spread
    if len(cuts) > 0:
        array = block_levels(rng, shape, cuts, -0.22, 0.18) * array
    return jnp.clip(array, min=-limit, max=limit).astype(kind)


def setup_inputs(seed: int = 0) -> dict:
    arg_keys = jax.random.split(jax.random.key(seed), 8)
    return {
        "propagator": scatter_about(arg_keys[0], (NSTN, M, M), M ** -0.5, 0.125, ((0, 16),)),
        "forcing": scatter_about(arg_keys[1], (NSTN, 2, NFREQ, M), 1.0, 6.0, ((0, 16), (2, 8))),
        "forward": scatter_about(arg_keys[2], (NSTN, 2, NFREQ, M), 1.0, 6.0, ((0, 16), (2, 8))),
        "damping": jnp.clip(jnp.exp(jax.random.uniform(arg_keys[3], (M,), jnp.float32, math.log(0.0005), math.log(0.05))), 0.0005, 0.05),
        "slowness": jnp.clip(jax.random.uniform(arg_keys[4], (M,), jnp.float32, 0.5, 2.0), 0.5, 2.0),
        "station_gap": with_ends(jax.random.randint(arg_keys[5], (NSTN,), 1, 4), jax.random.fold_in(arg_keys[5], 1), 1, 3).astype(jnp.int32),
        "freq_index": jax.random.permutation(arg_keys[6], NFREQ).astype(jnp.int32),
    }


frequency_step = 0.05

def reference(propagator, forcing, forward, damping, slowness, station_gap, freq_index):
    spacing = station_gap.astype(jnp.float32)
    frequency = frequency_step * (freq_index.astype(jnp.float32) + 1.0)
    state = forward.astype(jnp.float32)
    state_after = jnp.concatenate([state[1:], jnp.zeros((1, 2, NFREQ, M), jnp.float32)], axis=0)
    weighting = 1.0 / (4.0 * math.sqrt(NFREQ))

    def upstream_step(carried, inputs):
        operator_rows, forcing_here, state_here, state_next, spacing_here = inputs
        sent = carried.astype(jnp.bfloat16).reshape(2 * NFREQ, M)
        mixed = jnp.dot(sent, operator_rows, preferred_element_type=jnp.float32).reshape(2, NFREQ, M)
        damped = jnp.exp(-damping * spacing_here)
        angle = frequency[:, None] * (spacing_here * slowness)[None, :]
        cosine = damped * jnp.cos(angle)
        sine_part = damped * jnp.sin(angle)
        forcing_float = forcing_here.astype(jnp.float32)
        real_part = cosine * mixed[0] + sine_part * mixed[1] + forcing_float[0]
        imag_part = cosine * mixed[1] - sine_part * mixed[0] + forcing_float[1]
        adjoint = jnp.stack([real_part, imag_part])
        stream_slope = (state_next - state_here) / spacing_here
        profile = state_here.reshape(2, NFREQ, NVAR, NWALL)
        padded = jnp.pad(profile, ((0, 0), (0, 0), (0, 0), (1, 1)))
        normal_slope = (0.5 * (padded[..., 2:] - padded[..., :-2])).reshape(2, NFREQ, M)
        result = lax.optimization_barrier(jnp.sum(adjoint * (stream_slope + normal_slope), axis=(0, 1))) * weighting
        return (adjoint, result)
    start = jnp.zeros((2, NFREQ, M), jnp.float32)
    final, sensitivity = lax.scan(upstream_step, start, (propagator, forcing, state, state_after, spacing), reverse=True)
    return sensitivity
```

```python
import functools
import math

import jax
import jax.numpy as jnp
from jax import lax
from jax.experimental import pallas as pl
from jax.experimental.pallas import tpu as pltpu
from jax.sharding import PartitionSpec as P

NVAR = 5
BLOCKS = 2
PASS_ROWS = 128
TILE = 256
LANES = 128

frequency_step = 0.05

ON_CHIP = pl.BlockSpec(memory_space=pltpu.VMEM)
IN_PLACE = pl.BlockSpec(memory_space=pl.ANY)
SCALARS = pl.BlockSpec(memory_space=pltpu.SMEM)


def from_behind(value, axis, by):
    length = lax.axis_size(axis)
    pairs = [(i, i + by) for i in range(length) if 0 <= i + by < length]
    return lax.ppermute(value, axis, pairs)


def in_blocks(value, dim, length):
    dims = value.shape
    tiles = value.reshape(*dims[:dim], length, dims[dim] // length, *dims[dim + 1 :])
    return jnp.moveaxis(tiles, dim, 0)


def summed_on_arrival(value, axis, dim):
    length = lax.axis_size(axis)
    tiles = lax.all_to_all(in_blocks(value, dim, length), axis, 0, 0, tiled=True)
    return jnp.sum(tiles, axis=0)


def prepare_kernel(
    gap, forward, rim, cos_one, sin_one, cosine, sine, slope, wide,
):
    stations, _, freqs, width = forward.shape
    padded = wide.shape[1]
    wall = width // NVAR
    place = lax.rem(lax.broadcasted_iota(jnp.int32, (freqs, padded), 1), wall)
    has_next = place != wall - 1
    has_last = place != 0
    wide[...] = jnp.zeros_like(wide)
    c1 = cos_one[...]
    s1 = sin_one[...]
    for station in range(stations):
        gap_here = gap[station]
        c2 = c1 * c1 - s1 * s1
        s2 = 2.0 * (c1 * s1)
        c3 = c2 * c1 - s2 * s1
        s3 = c2 * s1 + s2 * c1
        cosine[station] = jnp.where(gap_here == 1, c1, jnp.where(gap_here == 2, c2, c3))
        sine[station] = jnp.where(gap_here == 1, s1, jnp.where(gap_here == 2, s2, s3))
        spacing = gap_here.astype(jnp.float32)
        for part in range(2):
            here = forward[station, part].astype(jnp.float32)
            if station + 1 < stations:
                after = forward[station + 1, part].astype(jnp.float32)
            else:
                after = rim[part].astype(jnp.float32)
            wide[:, :width] = here
            profile = wide[...]
            up = jnp.where(has_next, pltpu.roll(profile, padded - 1, 1), 0.0)
            down = jnp.where(has_last, pltpu.roll(profile, 1, 1), 0.0)
            normal = 0.5 * (up - down)
            slope[station, part] = (after - here) / spacing + normal[:, :width]


def prepare(gap, forward, rim, cos_one, sin_one):
    stations, parts, freqs, width = forward.shape
    padded = -(-width // LANES) * LANES
    return pl.pallas_call(
        prepare_kernel,
        out_shape=(
            jax.ShapeDtypeStruct((stations, freqs, width), jnp.float32),
            jax.ShapeDtypeStruct((stations, freqs, width), jnp.float32),
            jax.ShapeDtypeStruct((stations, parts, freqs, width), jnp.float32),
        ),
        in_specs=[SCALARS, ON_CHIP, ON_CHIP, ON_CHIP, ON_CHIP],
        out_specs=(ON_CHIP, ON_CHIP, ON_CHIP),
        scratch_shapes=[pltpu.VMEM((freqs, padded), jnp.float32)],
        compiler_params=pltpu.CompilerParams(vmem_limit_bytes=16 << 20),
        name="prepare",
    )(gap, forward, rim, cos_one, sin_one)


def march_kernel(
    turn, block, position, incoming, operator, cosine, sine, forcing, slope, sums_in,
    outgoing, sums, rows,
):
    stations, freqs, width = cosine.shape
    half = incoming.shape[0] // 2
    count = 2 * half
    low = block * half

    @pl.when(position[0] == turn)
    def _():
        rows[:, count:] = jnp.zeros_like(rows[:, count:])
        rows[0, :count] = incoming[...]

        def one(step, carried):
            station = stations - 1 - step
            source = lax.rem(step, 2)
            state = rows[source]
            for start in range(0, width, TILE):
                cut = pl.ds(start, min(TILE, width - start))
                mixed = jnp.dot(state, operator[station, :, cut], preferred_element_type=jnp.float32)
                mixed_re, mixed_im = mixed[:half], mixed[half:count]
                c = cosine[station, low : low + half, cut]
                s = sine[station, low : low + half, cut]
                real_part = c * mixed_re + s * mixed_im + forcing[station, 0, low : low + half, cut].astype(jnp.float32)
                imag_part = c * mixed_im - s * mixed_re + forcing[station, 1, low : low + half, cut].astype(jnp.float32)
                rows[1 - source, :half, cut] = real_part.astype(jnp.bfloat16)
                rows[1 - source, half:count, cut] = imag_part.astype(jnp.bfloat16)
                product = (
                    real_part * slope[station, 0, low : low + half, cut]
                    + imag_part * slope[station, 1, low : low + half, cut]
                )
                total = jnp.sum(product, axis=0, keepdims=True)
                if block > 0:
                    total = total + sums_in[pl.ds(station, 1), cut]
                sums[pl.ds(station, 1), cut] = total
            return carried

        lax.fori_loop(0, stations, one, 0)
        outgoing[...] = rows[stations % 2, :count]


def march(turn, block, position, incoming, operator, cosine, sine, forcing, slope, sums):
    width = incoming.shape[1]
    return pl.pallas_call(
        functools.partial(march_kernel, turn, block),
        out_shape=(
            jax.ShapeDtypeStruct(incoming.shape, incoming.dtype),
            jax.ShapeDtypeStruct(sums.shape, sums.dtype),
        ),
        in_specs=[SCALARS] + [ON_CHIP] * 7,
        out_specs=(ON_CHIP, ON_CHIP),
        scratch_shapes=[pltpu.VMEM((2, PASS_ROWS, width), jnp.bfloat16)],
        input_output_aliases={7: 1},
        compiler_params=pltpu.CompilerParams(vmem_limit_bytes=8 << 20),
        name="march",
    )(position, incoming, operator, cosine, sine, forcing, slope, sums)


def body(propagator, forcing, forward, damping, slowness, station_gap, freq_index):
    stations, _, width = propagator.shape
    freqs = forcing.shape[2]
    chain = lax.axis_size("stn")
    position = lax.axis_index("stn").astype(jnp.int32).reshape(1)
    frequency = frequency_step * (freq_index.astype(jnp.float32) + 1.0)
    rim = from_behind(forward[0], "stn", -1)
    damped = jnp.exp(-damping)
    angle = frequency[:, None] * slowness[None, :]
    cos_one = damped * jnp.cos(angle)
    sin_one = damped * jnp.sin(angle)
    cosine, sine, slope = prepare(station_gap, forward, rim, cos_one, sin_one)
    half = freqs // BLOCKS
    incoming = [jnp.zeros((2 * half, width), jnp.bfloat16)] * BLOCKS
    sums = jnp.zeros((stations, width), jnp.float32)
    for turn in range(chain):
        here = chain - 1 - turn
        outgoing = []
        for block in range(BLOCKS):
            out, sums = march(
                here, block, position, incoming[block],
                propagator, cosine, sine, forcing, slope, sums,
            )
            if here > 0:
                out = lax.ppermute(out, "stn", [(here, here - 1)])
            outgoing.append(out)
        incoming = outgoing
    weighting = 1.0 / (4.0 * math.sqrt(freqs * lax.axis_size("freq")))
    return summed_on_arrival(sums * weighting, "freq", 1)


def solution(mesh):
    placed = (
        P("stn", None, None),
        P("stn", None, "freq", None),
        P("stn", None, "freq", None),
        P(),
        P(),
        P("stn"),
        P("freq"),
    )
    return jax.shard_map(
        body, mesh=mesh, in_specs=placed, out_specs=P("stn", "freq"), check_vma=False
    )
```

```python
import functools
import math

import jax
import jax.numpy as jnp
from jax import lax
from jax.experimental import pallas as pl
from jax.experimental.pallas import tpu as pltpu
from jax.sharding import PartitionSpec as P

NVAR = 5
BLOCKS = 2
PASS_ROWS = 128
TILE = 256
LANES = 128

frequency_step = 0.05

ON_CHIP = pl.BlockSpec(memory_space=pltpu.VMEM)
IN_PLACE = pl.BlockSpec(memory_space=pl.ANY)
SCALARS = pl.BlockSpec(memory_space=pltpu.SMEM)


def from_behind(value, axis, by):
    length = lax.axis_size(axis)
    pairs = [(i, i + by) for i in range(length) if 0 <= i + by < length]
    return lax.ppermute(value, axis, pairs)


def in_blocks(value, dim, length):
    dims = value.shape
    tiles = value.reshape(*dims[:dim], length, dims[dim] // length, *dims[dim + 1 :])
    return jnp.moveaxis(tiles, dim, 0)


def summed_on_arrival(value, axis, dim):
    length = lax.axis_size(axis)
    tiles = lax.all_to_all(in_blocks(value, dim, length), axis, 0, 0, tiled=True)
    return jnp.sum(tiles, axis=0)


def prepare_kernel(
    gap, freq_index, forward, damping, slowness, cosine, sine, slope, angle, wide,
):
    stations, _, freqs, width = forward.shape
    padded = wide.shape[1]
    slow = slowness[...]
    for row in range(freqs):
        frequency = frequency_step * (freq_index[row].astype(jnp.float32) + 1.0)
        angle[row : row + 1, :] = frequency * slow
    damped = jnp.exp(-damping[...])
    c1 = damped * jnp.cos(angle[...])
    s1 = damped * jnp.sin(angle[...])
    wall = width // NVAR
    place = lax.rem(lax.broadcasted_iota(jnp.int32, (freqs, padded), 1), wall)
    has_next = place != wall - 1
    has_last = place != 0
    wide[...] = jnp.zeros_like(wide)
    for station in range(stations):
        gap_here = gap[station]
        c2 = c1 * c1 - s1 * s1
        s2 = 2.0 * (c1 * s1)
        c3 = c2 * c1 - s2 * s1
        s3 = c2 * s1 + s2 * c1
        cosine[station] = jnp.where(gap_here == 1, c1, jnp.where(gap_here == 2, c2, c3))
        sine[station] = jnp.where(gap_here == 1, s1, jnp.where(gap_here == 2, s2, s3))
        spacing = gap_here.astype(jnp.float32)
        for part in range(2):
            here = forward[station, part].astype(jnp.float32)
            wide[:, :width] = here
            profile = wide[...]
            up = jnp.where(has_next, pltpu.roll(profile, padded - 1, 1), 0.0)
            down = jnp.where(has_last, pltpu.roll(profile, 1, 1), 0.0)
            normal = (0.5 * (up - down))[:, :width]
            if station + 1 < stations:
                after = forward[station + 1, part].astype(jnp.float32)
                slope[station, part] = (after - here) / spacing + normal
            else:
                slope[station, part] = normal - here / spacing


def prepare(gap, freq_index, forward, damping, slowness):
    stations, parts, freqs, width = forward.shape
    padded = -(-width // LANES) * LANES
    return pl.pallas_call(
        prepare_kernel,
        out_shape=(
            pltpu.VMEM((stations, freqs, width), jnp.float32),
            pltpu.VMEM((stations, freqs, width), jnp.float32),
            pltpu.VMEM((stations, parts, freqs, width), jnp.float32),
        ),
        in_specs=[SCALARS, SCALARS, ON_CHIP, ON_CHIP, ON_CHIP],
        out_specs=(ON_CHIP, ON_CHIP, ON_CHIP),
        scratch_shapes=[pltpu.VMEM((freqs, width), jnp.float32), pltpu.VMEM((freqs, padded), jnp.float32)],
        cost_estimate=pl.CostEstimate(flops=16 << 30, bytes_accessed=64 << 20, transcendentals=0),
        compiler_params=pltpu.CompilerParams(vmem_limit_bytes=10 << 20),
        name="prepare",
    )(gap, freq_index, forward, damping, slowness)


def finish_kernel(gap, rim, slope_in, slope):
    del slope_in
    stations, parts, _, _ = slope.shape
    spacing = gap[stations - 1].astype(jnp.float32)
    for part in range(parts):
        slope[stations - 1, part] += rim[part].astype(jnp.float32) / spacing


def finish(gap, rim, slope):
    return pl.pallas_call(
        finish_kernel,
        out_shape=pltpu.VMEM(slope.shape, slope.dtype),
        in_specs=[SCALARS, ON_CHIP, ON_CHIP],
        out_specs=ON_CHIP,
        input_output_aliases={2: 0},
        compiler_params=pltpu.CompilerParams(vmem_limit_bytes=4 << 20),
        name="finish",
    )(gap, rim, pltpu.with_memory_space_constraint(slope, pltpu.VMEM))


def march_kernel(
    turn, block, incoming, operator, cosine, sine, forcing, slope, sums_in,
    outgoing, sums, rows,
):
    stations, freqs, width = cosine.shape
    half = incoming.shape[0] // 2
    count = 2 * half
    low = block * half

    @pl.when(lax.axis_index("stn") == turn)
    def _():
        rows[:, count:] = jnp.zeros_like(rows[:, count:])
        rows[0, :count] = incoming[...]

        def one(step, carried):
            station = stations - 1 - step
            source = lax.rem(step, 2)
            state = rows[source]
            for start in range(0, width, TILE):
                cut = pl.ds(start, min(TILE, width - start))
                mixed = jnp.dot(state, operator[station, :, cut], preferred_element_type=jnp.float32)
                mixed_re, mixed_im = mixed[:half], mixed[half:count]
                c = cosine[station, low : low + half, cut]
                s = sine[station, low : low + half, cut]
                real_part = c * mixed_re + s * mixed_im + forcing[station, 0, low : low + half, cut].astype(jnp.float32)
                imag_part = c * mixed_im - s * mixed_re + forcing[station, 1, low : low + half, cut].astype(jnp.float32)
                rows[1 - source, :half, cut] = real_part.astype(jnp.bfloat16)
                rows[1 - source, half:count, cut] = imag_part.astype(jnp.bfloat16)
                product = (
                    real_part * slope[station, 0, low : low + half, cut]
                    + imag_part * slope[station, 1, low : low + half, cut]
                )
                total = jnp.sum(product, axis=0, keepdims=True)
                if block > 0:
                    total = total + sums_in[pl.ds(station, 1), cut]
                sums[pl.ds(station, 1), cut] = total
            return carried

        lax.fori_loop(0, stations, one, 0)
        outgoing[...] = rows[stations % 2, :count]


def march(turn, block, incoming, operator, cosine, sine, forcing, slope, sums):
    held = [pltpu.with_memory_space_constraint(v, pltpu.VMEM) for v in (operator, cosine, sine, forcing, slope)]
    width = incoming.shape[1]
    return pl.pallas_call(
        functools.partial(march_kernel, turn, block),
        out_shape=(
            jax.ShapeDtypeStruct(incoming.shape, incoming.dtype),
            jax.ShapeDtypeStruct(sums.shape, sums.dtype),
        ),
        in_specs=[ON_CHIP] * 7,
        out_specs=(ON_CHIP, ON_CHIP),
        scratch_shapes=[pltpu.VMEM((2, PASS_ROWS, width), jnp.bfloat16)],
        input_output_aliases={6: 1},
        compiler_params=pltpu.CompilerParams(vmem_limit_bytes=4 << 20),
        name="march",
    )(incoming, *held, sums)


def body(propagator, forcing, forward, damping, slowness, station_gap, freq_index):
    stations, _, width = propagator.shape
    freqs = forcing.shape[2]
    chain = lax.axis_size("stn")
    rim = from_behind(forward[0], "stn", -1)
    cosine, sine, slope = prepare(
        station_gap, freq_index, forward, damping[None, :], slowness[None, :]
    )
    slope = finish(station_gap, rim, slope)
    half = freqs // BLOCKS
    incoming = [jnp.zeros((2 * half, width), jnp.bfloat16)] * BLOCKS
    sums = jnp.zeros((stations, width), jnp.float32)
    for turn in range(chain):
        here = chain - 1 - turn
        outgoing = []
        for block in range(BLOCKS):
            out, sums = march(
                here, block, incoming[block],
                propagator, cosine, sine, forcing, slope, sums,
            )
            if here > 0:
                out = lax.ppermute(out, "stn", [(here, here - 1)])
            outgoing.append(out)
        incoming = outgoing
    weighting = 1.0 / (4.0 * math.sqrt(freqs * lax.axis_size("freq")))
    return summed_on_arrival(sums * weighting, "freq", 1)


def solution(mesh):
    placed = (
        P("stn", None, None),
        P("stn", None, "freq", None),
        P("stn", None, "freq", None),
        P(),
        P(),
        P("stn"),
        P("freq"),
    )
    return jax.shard_map(
        body, mesh=mesh, in_specs=placed, out_specs=P("stn", "freq"), check_vma=False
    )
```

```python
import functools
import math

import jax
import jax.numpy as jnp
from jax import lax
from jax.experimental import pallas as pl
from jax.experimental.pallas import tpu as pltpu
from jax.sharding import PartitionSpec as P

NVAR = 5
BLOCKS = 2
PASS_ROWS = 128
TILE = 256
LANES = 128

frequency_step = 0.05

ON_CHIP = pl.BlockSpec(memory_space=pltpu.VMEM)
IN_PLACE = pl.BlockSpec(memory_space=pl.ANY)
SCALARS = pl.BlockSpec(memory_space=pltpu.SMEM)


def from_behind(value, axis, by):
    length = lax.axis_size(axis)
    pairs = [(i, i + by) for i in range(length) if 0 <= i + by < length]
    return lax.ppermute(value, axis, pairs)


def in_blocks(value, dim, length):
    dims = value.shape
    tiles = value.reshape(*dims[:dim], length, dims[dim] // length, *dims[dim + 1 :])
    return jnp.moveaxis(tiles, dim, 0)


def summed_on_arrival(value, axis, dim):
    length = lax.axis_size(axis)
    tiles = lax.all_to_all(in_blocks(value, dim, length), axis, 0, 0, tiled=True)
    return jnp.sum(tiles, axis=0)


def prepare_kernel(
    gap_hbm, freq_index_hbm, forward_hbm, damping_hbm, slowness_hbm,
    cosine, sine, slope, edge,
    angle, wide, gap, freq_index, forward, damping, slowness, arrived,
):
    stations, _, freqs, width = forward.shape
    padded = wide.shape[1]
    fetches = [
        pltpu.make_async_copy(source, target, arrived.at[i])
        for i, (source, target) in enumerate((
            (freq_index_hbm, freq_index), (slowness_hbm, slowness), (damping_hbm, damping),
            (gap_hbm, gap), (forward_hbm, forward),
        ))
    ]
    for fetch in fetches:
        fetch.start()
    wide[...] = jnp.zeros_like(wide)
    for fetch in fetches[:4]:
        fetch.wait()
    slow = slowness[...]
    for row in range(freqs):
        frequency = frequency_step * (freq_index[row].astype(jnp.float32) + 1.0)
        angle[row : row + 1, :] = frequency * slow
    damped = jnp.exp(-damping[...])
    c1 = damped * jnp.cos(angle[...])
    s1 = damped * jnp.sin(angle[...])
    wall = width // NVAR
    place = lax.rem(lax.broadcasted_iota(jnp.int32, (freqs, padded), 1), wall)
    has_next = place != wall - 1
    has_last = place != 0
    fetches[4].wait()
    edge[...] = forward[0]
    for station in range(stations):
        gap_here = gap[station]
        c2 = c1 * c1 - s1 * s1
        s2 = 2.0 * (c1 * s1)
        c3 = c2 * c1 - s2 * s1
        s3 = c2 * s1 + s2 * c1
        cosine[station] = jnp.where(gap_here == 1, c1, jnp.where(gap_here == 2, c2, c3))
        sine[station] = jnp.where(gap_here == 1, s1, jnp.where(gap_here == 2, s2, s3))
        spacing = gap_here.astype(jnp.float32)
        for part in range(2):
            here = forward[station, part].astype(jnp.float32)
            wide[:, :width] = here
            profile = wide[...]
            up = jnp.where(has_next, pltpu.roll(profile, padded - 1, 1), 0.0)
            down = jnp.where(has_last, pltpu.roll(profile, 1, 1), 0.0)
            normal = (0.5 * (up - down))[:, :width]
            if station + 1 < stations:
                after = forward[station + 1, part].astype(jnp.float32)
                slope[station, part] = (after - here) / spacing + normal
            else:
                slope[station, part] = normal - here / spacing


def prepare(gap, freq_index, forward, damping, slowness):
    stations, parts, freqs, width = forward.shape
    padded = -(-width // LANES) * LANES
    return pl.pallas_call(
        prepare_kernel,
        out_shape=(
            pltpu.VMEM((stations, freqs, width), jnp.float32),
            pltpu.VMEM((stations, freqs, width), jnp.float32),
            pltpu.VMEM((stations, parts, freqs, width), jnp.float32),
            jax.ShapeDtypeStruct((parts, freqs, width), forward.dtype),
        ),
        in_specs=[IN_PLACE] * 5,
        out_specs=(ON_CHIP,) * 4,
        scratch_shapes=[
            pltpu.VMEM((freqs, width), jnp.float32),
            pltpu.VMEM((freqs, padded), jnp.float32),
            pltpu.SMEM(gap.shape, gap.dtype),
            pltpu.SMEM(freq_index.shape, freq_index.dtype),
            pltpu.VMEM(forward.shape, forward.dtype),
            pltpu.VMEM(damping.shape, damping.dtype),
            pltpu.VMEM(slowness.shape, slowness.dtype),
            pltpu.SemaphoreType.DMA((5,)),
        ],
        cost_estimate=pl.CostEstimate(flops=16 << 30, bytes_accessed=64 << 20, transcendentals=0),
        compiler_params=pltpu.CompilerParams(vmem_limit_bytes=10 << 20),
        name="prepare",
    )(*[pltpu.with_memory_space_constraint(v, pltpu.HBM) for v in (gap, freq_index, forward, damping, slowness)])


def finish_kernel(gap, rim, slope_in, after, slope):
    del slope_in, after
    stations, parts, _, _ = slope.shape
    spacing = gap[stations - 1].astype(jnp.float32)
    for part in range(parts):
        slope[stations - 1, part] += rim[part].astype(jnp.float32) / spacing


def finish(gap, rim, slope, after):
    return pl.pallas_call(
        finish_kernel,
        out_shape=pltpu.VMEM(slope.shape, slope.dtype),
        in_specs=[SCALARS, ON_CHIP, ON_CHIP, IN_PLACE],
        out_specs=ON_CHIP,
        input_output_aliases={2: 0},
        compiler_params=pltpu.CompilerParams(vmem_limit_bytes=4 << 20),
        name="finish",
    )(gap, rim, pltpu.with_memory_space_constraint(slope, pltpu.VMEM), after)


def march_kernel(
    turn, block, first, incoming, operator, cosine, sine, forcing, slope, sums_in,
    outgoing, sums, rows,
):
    stations, freqs, width = cosine.shape
    half = incoming.shape[0] // 2
    count = 2 * half
    low = block * half

    @pl.when(lax.axis_index("stn") == turn)
    def _():
        rows[:, count:] = jnp.zeros_like(rows[:, count:])

        def settle(station, target, cut, mixed):
            real_part = forcing[station, 0, low : low + half, cut].astype(jnp.float32)
            imag_part = forcing[station, 1, low : low + half, cut].astype(jnp.float32)
            if mixed is not None:
                mixed_re, mixed_im = mixed[:half], mixed[half:count]
                c = cosine[station, low : low + half, cut]
                s = sine[station, low : low + half, cut]
                real_part = c * mixed_re + s * mixed_im + real_part
                imag_part = c * mixed_im - s * mixed_re + imag_part
            rows[target, :half, cut] = real_part.astype(jnp.bfloat16)
            rows[target, half:count, cut] = imag_part.astype(jnp.bfloat16)
            product = (
                real_part * slope[station, 0, low : low + half, cut]
                + imag_part * slope[station, 1, low : low + half, cut]
            )
            total = jnp.sum(product, axis=0, keepdims=True)
            if block > 0:
                total = total + sums_in[pl.ds(station, 1), cut]
            sums[pl.ds(station, 1), cut] = total

        def one(step, carried):
            station = stations - 1 - step
            source = lax.rem(step, 2)
            state = rows[source]
            for start in range(0, width, TILE):
                cut = pl.ds(start, min(TILE, width - start))
                mixed = jnp.dot(state, operator[station, :, cut], preferred_element_type=jnp.float32)
                settle(station, 1 - source, cut, mixed)
            return carried

        if first:
            for start in range(0, width, TILE):
                settle(stations - 1, 1, pl.ds(start, min(TILE, width - start)), None)
            lax.fori_loop(1, stations, one, 0)
        else:
            rows[0, :count] = incoming[...]
            lax.fori_loop(0, stations, one, 0)
        outgoing[...] = rows[stations % 2, :count]


def march(turn, block, first, incoming, operator, cosine, sine, forcing, slope, sums):
    held = [pltpu.with_memory_space_constraint(v, pltpu.VMEM) for v in (operator, cosine, sine, forcing, slope)]
    width = incoming.shape[1]
    return pl.pallas_call(
        functools.partial(march_kernel, turn, block, first),
        out_shape=(
            jax.ShapeDtypeStruct(incoming.shape, incoming.dtype),
            jax.ShapeDtypeStruct(sums.shape, sums.dtype),
        ),
        in_specs=[ON_CHIP] * 7,
        out_specs=(ON_CHIP, ON_CHIP),
        scratch_shapes=[pltpu.VMEM((2, PASS_ROWS, width), jnp.bfloat16)],
        input_output_aliases={6: 1},
        compiler_params=pltpu.CompilerParams(vmem_limit_bytes=4 << 20),
        name="march",
    )(incoming, *held, sums)


def body(propagator, forcing, forward, damping, slowness, station_gap, freq_index):
    stations, _, width = propagator.shape
    freqs = forcing.shape[2]
    chain = lax.axis_size("stn")
    cosine, sine, slope, edge = prepare(
        station_gap, freq_index, forward, damping[None, :], slowness[None, :]
    )
    half = freqs // BLOCKS
    incoming = [jnp.zeros((2 * half, width), jnp.bfloat16)] * BLOCKS
    sums = jnp.zeros((stations, width), jnp.float32)
    for turn in range(chain):
        here = chain - 1 - turn
        outgoing = []
        for block in range(BLOCKS):
            out, sums = march(
                here, block, turn == 0, incoming[block],
                propagator, cosine, sine, forcing, slope, sums,
            )
            if here > 0:
                out = lax.ppermute(out, "stn", [(here, here - 1)])
            outgoing.append(out)
        incoming = outgoing
        if turn == 0:
            rim = from_behind(edge, "stn", -1)
            slope = finish(station_gap, rim, slope, sums)
    weighting = 1.0 / (4.0 * math.sqrt(freqs * lax.axis_size("freq")))
    return summed_on_arrival(sums * weighting, "freq", 1)


def solution(mesh):
    placed = (
        P("stn", None, None),
        P("stn", None, "freq", None),
        P("stn", None, "freq", None),
        P(),
        P(),
        P("stn"),
        P("freq"),
    )
    return jax.shard_map(
        body, mesh=mesh, in_specs=placed, out_specs=P("stn", "freq"), check_vma=False
    )
```

```python
import functools
import math

import jax
import jax.numpy as jnp
from jax import lax
from jax.experimental import pallas as pl
from jax.experimental.pallas import tpu as pltpu
from jax.sharding import PartitionSpec as P

NVAR = 5
BLOCKS = 2
PASS_ROWS = 128
TILE = 256
UNITS = 2
LANES = 128

frequency_step = 0.05

ON_CHIP = pl.BlockSpec(memory_space=pltpu.VMEM)
IN_PLACE = pl.BlockSpec(memory_space=pl.ANY)
SCALARS = pl.BlockSpec(memory_space=pltpu.SMEM)


def from_behind(value, axis, by):
    length = lax.axis_size(axis)
    pairs = [(i, i + by) for i in range(length) if 0 <= i + by < length]
    return lax.ppermute(value, axis, pairs)


def in_blocks(value, dim, length):
    dims = value.shape
    tiles = value.reshape(*dims[:dim], length, dims[dim] // length, *dims[dim + 1 :])
    return jnp.moveaxis(tiles, dim, 0)


def summed_on_arrival(value, axis, dim):
    length = lax.axis_size(axis)
    tiles = lax.all_to_all(in_blocks(value, dim, length), axis, 0, 0, tiled=True)
    return jnp.sum(tiles, axis=0)


def prepare_kernel(
    gap_hbm, freq_index_hbm, forward_hbm, damping_hbm, slowness_hbm,
    cosine, sine, slope, edge,
    angle, wide, gap, freq_index, forward, damping, slowness, arrived,
):
    stations, _, freqs, width = forward.shape
    padded = wide.shape[1]
    fetches = [
        pltpu.make_async_copy(source, target, arrived.at[i])
        for i, (source, target) in enumerate((
            (freq_index_hbm, freq_index), (slowness_hbm, slowness), (damping_hbm, damping),
            (gap_hbm, gap), (forward_hbm, forward),
        ))
    ]
    for fetch in fetches:
        fetch.start()
    wide[...] = jnp.zeros_like(wide)
    for fetch in fetches[:4]:
        fetch.wait()
    slow = slowness[...]
    for row in range(freqs):
        frequency = frequency_step * (freq_index[row].astype(jnp.float32) + 1.0)
        angle[row : row + 1, :] = frequency * slow
    damped = jnp.exp(-damping[...])
    c1 = damped * jnp.cos(angle[...])
    s1 = damped * jnp.sin(angle[...])
    wall = width // NVAR
    place = lax.rem(lax.broadcasted_iota(jnp.int32, (freqs, padded), 1), wall)
    has_next = place != wall - 1
    has_last = place != 0
    fetches[4].wait()
    edge[...] = forward[0]
    for station in range(stations):
        gap_here = gap[station]
        c2 = c1 * c1 - s1 * s1
        s2 = 2.0 * (c1 * s1)
        c3 = c2 * c1 - s2 * s1
        s3 = c2 * s1 + s2 * c1
        cosine[station] = jnp.where(gap_here == 1, c1, jnp.where(gap_here == 2, c2, c3))
        sine[station] = jnp.where(gap_here == 1, s1, jnp.where(gap_here == 2, s2, s3))
        spacing = gap_here.astype(jnp.float32)
        for part in range(2):
            here = forward[station, part].astype(jnp.float32)
            wide[:, :width] = here
            profile = wide[...]
            up = jnp.where(has_next, pltpu.roll(profile, padded - 1, 1), 0.0)
            down = jnp.where(has_last, pltpu.roll(profile, 1, 1), 0.0)
            normal = (0.5 * (up - down))[:, :width]
            if station + 1 < stations:
                after = forward[station + 1, part].astype(jnp.float32)
                slope[station, part] = (after - here) / spacing + normal
            else:
                slope[station, part] = normal - here / spacing


def prepare(gap, freq_index, forward, damping, slowness):
    stations, parts, freqs, width = forward.shape
    padded = -(-width // LANES) * LANES
    return pl.pallas_call(
        prepare_kernel,
        out_shape=(
            pltpu.VMEM((stations, freqs, width), jnp.float32),
            pltpu.VMEM((stations, freqs, width), jnp.float32),
            pltpu.VMEM((stations, parts, freqs, width), jnp.float32),
            jax.ShapeDtypeStruct((parts, freqs, width), forward.dtype),
        ),
        in_specs=[IN_PLACE] * 5,
        out_specs=(ON_CHIP,) * 4,
        scratch_shapes=[
            pltpu.VMEM((freqs, width), jnp.float32),
            pltpu.VMEM((freqs, padded), jnp.float32),
            pltpu.SMEM(gap.shape, gap.dtype),
            pltpu.SMEM(freq_index.shape, freq_index.dtype),
            pltpu.VMEM(forward.shape, forward.dtype),
            pltpu.VMEM(damping.shape, damping.dtype),
            pltpu.VMEM(slowness.shape, slowness.dtype),
            pltpu.SemaphoreType.DMA((5,)),
        ],
        cost_estimate=pl.CostEstimate(flops=16 << 30, bytes_accessed=64 << 20, transcendentals=0),
        compiler_params=pltpu.CompilerParams(vmem_limit_bytes=10 << 20),
        name="prepare",
    )(*[pltpu.with_memory_space_constraint(v, pltpu.HBM) for v in (gap, freq_index, forward, damping, slowness)])


def finish_kernel(gap, rim, slope_in, after, slope):
    del slope_in, after
    stations, parts, _, _ = slope.shape
    spacing = gap[stations - 1].astype(jnp.float32)
    for part in range(parts):
        slope[stations - 1, part] += rim[part].astype(jnp.float32) / spacing


def finish(gap, rim, slope, after):
    return pl.pallas_call(
        finish_kernel,
        out_shape=pltpu.VMEM(slope.shape, slope.dtype),
        in_specs=[SCALARS, ON_CHIP, ON_CHIP, IN_PLACE],
        out_specs=ON_CHIP,
        input_output_aliases={2: 0},
        compiler_params=pltpu.CompilerParams(vmem_limit_bytes=4 << 20),
        name="finish",
    )(gap, rim, pltpu.with_memory_space_constraint(slope, pltpu.VMEM), after)


def march_kernel(
    turn, block, first, incoming, operator, cosine, sine, forcing, slope, sums_in, *results,
):
    sums, outgoing, rows = results[0], results[1:-1], results[-1]
    stations, freqs, width = cosine.shape
    half = incoming.shape[0] // 2
    count = 2 * half
    low = block * half
    full = width // TILE
    rest = width - full * TILE
    tiles = full + 1
    groups = tiles // UNITS
    edge = width // LANES * LANES

    def settle(station, tile, mixed):
        start = tile * TILE
        size = min(TILE, width - start)
        cut = slice(start, start + size)
        real_part = forcing[station, 0, low : low + half, cut].astype(jnp.float32)
        imag_part = forcing[station, 1, low : low + half, cut].astype(jnp.float32)
        if mixed is not None:
            mixed_re, mixed_im = mixed[:half, :size], mixed[half:count, :size]
            c = cosine[station, low : low + half, cut]
            s = sine[station, low : low + half, cut]
            real_part = c * mixed_re + s * mixed_im + real_part
            imag_part = c * mixed_im - s * mixed_re + imag_part
        rows[:half, cut] = real_part.astype(jnp.bfloat16)
        rows[half:count, cut] = imag_part.astype(jnp.bfloat16)
        product = (
            real_part * slope[station, 0, low : low + half, cut]
            + imag_part * slope[station, 1, low : low + half, cut]
        )
        total = jnp.sum(product, axis=0, keepdims=True)
        if block > 0:
            total = total + sums_in[pl.ds(station, 1), cut]
        sums[pl.ds(station, 1), cut] = total

    def run(*sums_of):
        def one(step, carried):
            station = stations - 1 - step

            def piece(depth, tile):
                deep = slice(full * TILE, width)
                if not (isinstance(depth, int) and depth == full):
                    deep = pl.ds(pl.multiple_of(depth * TILE, TILE), TILE)
                cut = slice(tile * TILE, min((tile + 1) * TILE, width))
                value = operator[station, deep, cut]
                if value.shape[1] < TILE:
                    blank = jnp.zeros((value.shape[0], TILE - rest), value.dtype)
                    value = jnp.concatenate([value, blank], axis=1)
                if value.shape[0] < TILE:
                    blank = jnp.zeros((TILE - rest, TILE), value.dtype)
                    value = jnp.concatenate([value, blank], axis=0)
                return value

            def push(depth, group):
                for unit in range(UNITS):
                    pltpu.matmul_push_rhs(piece(depth, UNITS * group + unit), group % 2, unit)

            def state_at(depth):
                return rows[:, pl.ds(pl.multiple_of(depth * TILE, TILE), TILE)]

            def accumulate(state, group):
                for unit in range(UNITS):
                    pltpu.matmul_acc_lhs(sums_of[UNITS * group + unit], state, load_staged_rhs=group % 2)

            def deepen(depth, carried):
                state = state_at(depth)
                for group in range(groups):
                    if group + 1 < groups:
                        push(depth, group + 1)
                    else:
                        push(depth + 1, 0)
                    accumulate(state, group)
                return carried

            push(0, 0)
            lax.fori_loop(0, full - 1, deepen, 0)
            deepen(full - 1, 0)
            state = rows[:, full * TILE :]
            for group in range(groups):
                if group + 1 < groups:
                    push(full, group + 1)
                accumulate(state, group)
            for tile in range(tiles):
                settle(station, tile, pltpu.matmul_pop(sums_of[tile]))
            return carried

        rows[:count, edge:] = jnp.zeros_like(rows[:count, edge:])
        if first:
            for tile in range(tiles):
                settle(stations - 1, tile, None)
            lax.fori_loop(1, stations, one, 0)
        else:
            rows[:count, :width] = incoming[...]
            lax.fori_loop(0, stations, one, 0)
        for out in outgoing:
            out[...] = rows[:count, :width]

    @pl.when(lax.axis_index("stn") == turn)
    def _():
        pl.run_scoped(
            run, *[pltpu.ACC(tile % UNITS)((PASS_ROWS, TILE), jnp.float32) for tile in range(tiles)]
        )


def march(turn, block, first, incoming, operator, cosine, sine, forcing, slope, sums):
    held = [pltpu.with_memory_space_constraint(v, pltpu.VMEM) for v in (operator, cosine, sine, forcing, slope)]
    padded = -(-incoming.shape[1] // TILE) * TILE
    results = [jax.ShapeDtypeStruct(sums.shape, sums.dtype)]
    if turn > 0:
        results.append(jax.ShapeDtypeStruct(incoming.shape, incoming.dtype))
    return pl.pallas_call(
        functools.partial(march_kernel, turn, block, first),
        out_shape=results,
        in_specs=[ON_CHIP] * 7,
        out_specs=[ON_CHIP] * len(results),
        scratch_shapes=[pltpu.VMEM((PASS_ROWS, padded), jnp.bfloat16)],
        input_output_aliases={6: 0},
        compiler_params=pltpu.CompilerParams(vmem_limit_bytes=4 << 20),
        name="march",
    )(incoming, *held, sums)


def body(propagator, forcing, forward, damping, slowness, station_gap, freq_index):
    stations, _, width = propagator.shape
    freqs = forcing.shape[2]
    chain = lax.axis_size("stn")
    cosine, sine, slope, edge = prepare(
        station_gap, freq_index, forward, damping[None, :], slowness[None, :]
    )
    half = freqs // BLOCKS
    incoming = [jnp.zeros((2 * half, width), jnp.bfloat16)] * BLOCKS
    sums = jnp.zeros((stations, width), jnp.float32)
    for turn in range(chain):
        here = chain - 1 - turn
        outgoing = []
        for block in range(BLOCKS):
            sums, *out = march(
                here, block, turn == 0, incoming[block],
                propagator, cosine, sine, forcing, slope, sums,
            )
            outgoing += [lax.ppermute(v, "stn", [(here, here - 1)]) for v in out]
        incoming = outgoing
        if turn == 0:
            rim = from_behind(edge, "stn", -1)
            slope = finish(station_gap, rim, slope, sums)
    weighting = 1.0 / (4.0 * math.sqrt(freqs * lax.axis_size("freq")))
    return summed_on_arrival(sums * weighting, "freq", 1)


def solution(mesh):
    placed = (
        P("stn", None, None),
        P("stn", None, "freq", None),
        P("stn", None, "freq", None),
        P(),
        P(),
        P("stn"),
        P("freq"),
    )
    with jax.sharding.use_abstract_mesh(mesh.abstract_mesh):
        return jax.shard_map(
            body, mesh=mesh, in_specs=placed, out_specs=P("stn", "freq"), check_vma=False
        )
```

```python
import functools
import math

import jax
import jax.numpy as jnp
from jax import lax
from jax.experimental import pallas as pl
from jax.experimental.pallas import tpu as pltpu
from jax.sharding import PartitionSpec as P

NVAR = 5
BLOCKS = 2
PASS_ROWS = 128
TILE = 256
UNITS = 2
LANES = 128

frequency_step = 0.05

ON_CHIP = pl.BlockSpec(memory_space=pltpu.VMEM)
IN_PLACE = pl.BlockSpec(memory_space=pl.ANY)
SCALARS = pl.BlockSpec(memory_space=pltpu.SMEM)


def from_next(value, parity):
    pairs = [(i, i - 1) for i in range(1, lax.axis_size("stn")) if i % 2 == parity]
    return lax.ppermute(value, "stn", pairs)


def in_blocks(value, dim, length):
    dims = value.shape
    tiles = value.reshape(*dims[:dim], length, dims[dim] // length, *dims[dim + 1 :])
    return jnp.moveaxis(tiles, dim, 0)


def summed_on_arrival(value, axis, dim):
    length = lax.axis_size(axis)
    tiles = lax.all_to_all(in_blocks(value, dim, length), axis, 0, 0, tiled=True)
    return jnp.sum(tiles, axis=0)


def prepare_kernel(
    gap_hbm, freq_index_hbm, forward_hbm, damping_hbm, slowness_hbm,
    cosine, sine, slope, edge,
    angle, wide, gap, freq_index, forward, damping, slowness, arrived,
):
    stations, _, freqs, width = forward.shape
    padded = wide.shape[1]
    fetches = [
        pltpu.make_async_copy(source, target, arrived.at[i])
        for i, (source, target) in enumerate((
            (freq_index_hbm, freq_index), (slowness_hbm, slowness), (damping_hbm, damping),
            (gap_hbm, gap), (forward_hbm, forward),
        ))
    ]
    for fetch in fetches:
        fetch.start()
    wide[...] = jnp.zeros_like(wide)
    for fetch in fetches[:4]:
        fetch.wait()
    slow = slowness[...]
    for row in range(freqs):
        frequency = frequency_step * (freq_index[row].astype(jnp.float32) + 1.0)
        angle[row : row + 1, :] = frequency * slow
    damped = jnp.exp(-damping[...])
    c1 = damped * jnp.cos(angle[...])
    s1 = damped * jnp.sin(angle[...])
    wall = width // NVAR
    place = lax.rem(lax.broadcasted_iota(jnp.int32, (freqs, padded), 1), wall)
    has_next = place != wall - 1
    has_last = place != 0
    fetches[4].wait()
    edge[...] = forward[0]
    for station in range(stations):
        gap_here = gap[station]
        c2 = c1 * c1 - s1 * s1
        s2 = 2.0 * (c1 * s1)
        c3 = c2 * c1 - s2 * s1
        s3 = c2 * s1 + s2 * c1
        cosine[station] = jnp.where(gap_here == 1, c1, jnp.where(gap_here == 2, c2, c3))
        sine[station] = jnp.where(gap_here == 1, s1, jnp.where(gap_here == 2, s2, s3))
        spacing = gap_here.astype(jnp.float32)
        for part in range(2):
            here = forward[station, part].astype(jnp.float32)
            wide[:, :width] = here
            profile = wide[...]
            up = jnp.where(has_next, pltpu.roll(profile, padded - 1, 1), 0.0)
            down = jnp.where(has_last, pltpu.roll(profile, 1, 1), 0.0)
            normal = (0.5 * (up - down))[:, :width]
            if station + 1 < stations:
                after = forward[station + 1, part].astype(jnp.float32)
                slope[station, part] = (after - here) / spacing + normal
            else:
                slope[station, part] = normal - here / spacing


def prepare(gap, freq_index, forward, damping, slowness):
    stations, parts, freqs, width = forward.shape
    padded = -(-width // LANES) * LANES
    return pl.pallas_call(
        prepare_kernel,
        out_shape=(
            pltpu.VMEM((stations, freqs, width), jnp.float32),
            pltpu.VMEM((stations, freqs, width), jnp.float32),
            pltpu.VMEM((stations, parts, freqs, width), jnp.float32),
            jax.ShapeDtypeStruct((parts, freqs, width), forward.dtype),
        ),
        in_specs=[IN_PLACE] * 5,
        out_specs=(ON_CHIP,) * 4,
        scratch_shapes=[
            pltpu.VMEM((freqs, width), jnp.float32),
            pltpu.VMEM((freqs, padded), jnp.float32),
            pltpu.SMEM(gap.shape, gap.dtype),
            pltpu.SMEM(freq_index.shape, freq_index.dtype),
            pltpu.VMEM(forward.shape, forward.dtype),
            pltpu.VMEM(damping.shape, damping.dtype),
            pltpu.VMEM(slowness.shape, slowness.dtype),
            pltpu.SemaphoreType.DMA((5,)),
        ],
        cost_estimate=pl.CostEstimate(flops=16 << 30, bytes_accessed=64 << 20, transcendentals=0),
        compiler_params=pltpu.CompilerParams(vmem_limit_bytes=10 << 20),
        name="prepare",
    )(*[pltpu.with_memory_space_constraint(v, pltpu.HBM) for v in (gap, freq_index, forward, damping, slowness)])


def finish_kernel(gap, rim, slope_in, after, slope):
    del slope_in, after
    stations, parts, _, _ = slope.shape
    spacing = gap[stations - 1].astype(jnp.float32)
    for part in range(parts):
        slope[stations - 1, part] += rim[part].astype(jnp.float32) / spacing


def finish(gap, rim, slope, after):
    return pl.pallas_call(
        finish_kernel,
        out_shape=pltpu.VMEM(slope.shape, slope.dtype),
        in_specs=[SCALARS, ON_CHIP, ON_CHIP, IN_PLACE],
        out_specs=ON_CHIP,
        input_output_aliases={2: 0},
        compiler_params=pltpu.CompilerParams(vmem_limit_bytes=4 << 20),
        name="finish",
    )(gap, rim, pltpu.with_memory_space_constraint(slope, pltpu.VMEM), after)


def march_kernel(
    turn, block, first, incoming, operator, cosine, sine, forcing, slope, sums_in, *results,
):
    sums, outgoing, rows = results[0], results[1:-1], results[-1]
    stations, freqs, width = cosine.shape
    half = incoming.shape[0] // 2
    count = 2 * half
    low = block * half
    full = width // TILE
    rest = width - full * TILE
    tiles = full + 1
    groups = tiles // UNITS
    edge = width // LANES * LANES

    def settle(station, tile, mixed):
        start = tile * TILE
        size = min(TILE, width - start)
        cut = slice(start, start + size)
        real_part = forcing[station, 0, low : low + half, cut].astype(jnp.float32)
        imag_part = forcing[station, 1, low : low + half, cut].astype(jnp.float32)
        if mixed is not None:
            mixed_re, mixed_im = mixed[:half, :size], mixed[half:count, :size]
            c = cosine[station, low : low + half, cut]
            s = sine[station, low : low + half, cut]
            real_part = c * mixed_re + s * mixed_im + real_part
            imag_part = c * mixed_im - s * mixed_re + imag_part
        rows[:half, cut] = real_part.astype(jnp.bfloat16)
        rows[half:count, cut] = imag_part.astype(jnp.bfloat16)
        product = (
            real_part * slope[station, 0, low : low + half, cut]
            + imag_part * slope[station, 1, low : low + half, cut]
        )
        total = jnp.sum(product, axis=0, keepdims=True)
        if block > 0:
            total = total + sums_in[pl.ds(station, 1), cut]
        sums[pl.ds(station, 1), cut] = total

    def run(*sums_of):
        def one(step, carried):
            station = stations - 1 - step

            def piece(depth, tile):
                deep = slice(full * TILE, width)
                if not (isinstance(depth, int) and depth == full):
                    deep = pl.ds(pl.multiple_of(depth * TILE, TILE), TILE)
                cut = slice(tile * TILE, min((tile + 1) * TILE, width))
                value = operator[station, deep, cut]
                if value.shape[1] < TILE:
                    blank = jnp.zeros((value.shape[0], TILE - rest), value.dtype)
                    value = jnp.concatenate([value, blank], axis=1)
                if value.shape[0] < TILE:
                    blank = jnp.zeros((TILE - rest, TILE), value.dtype)
                    value = jnp.concatenate([value, blank], axis=0)
                return value

            def push(depth, group):
                for unit in range(UNITS):
                    pltpu.matmul_push_rhs(piece(depth, UNITS * group + unit), group % 2, unit)

            def state_at(depth):
                return rows[:, pl.ds(pl.multiple_of(depth * TILE, TILE), TILE)]

            def accumulate(state, group):
                for unit in range(UNITS):
                    pltpu.matmul_acc_lhs(sums_of[UNITS * group + unit], state, load_staged_rhs=group % 2)

            def deepen(depth, carried):
                state = state_at(depth)
                for group in range(groups):
                    if group + 1 < groups:
                        push(depth, group + 1)
                    else:
                        push(depth + 1, 0)
                    accumulate(state, group)
                return carried

            push(0, 0)
            lax.fori_loop(0, full - 1, deepen, 0)
            deepen(full - 1, 0)
            state = rows[:, full * TILE :]
            for group in range(groups):
                if group + 1 < groups:
                    push(full, group + 1)
                accumulate(state, group)
            for tile in range(tiles):
                settle(station, tile, pltpu.matmul_pop(sums_of[tile]))
            return carried

        rows[:count, edge:] = jnp.zeros_like(rows[:count, edge:])
        if first:
            for tile in range(tiles):
                settle(stations - 1, tile, None)
            lax.fori_loop(1, stations, one, 0)
        else:
            rows[:count, :width] = incoming[...]
            lax.fori_loop(0, stations, one, 0)
        for out in outgoing:
            out[...] = rows[:count, :width]

    @pl.when(lax.axis_index("stn") == turn)
    def _():
        pl.run_scoped(
            run, *[pltpu.ACC(tile % UNITS)((PASS_ROWS, TILE), jnp.float32) for tile in range(tiles)]
        )


def march(turn, block, first, incoming, operator, cosine, sine, forcing, slope, sums):
    held = [pltpu.with_memory_space_constraint(v, pltpu.VMEM) for v in (operator, cosine, sine, forcing, slope)]
    padded = -(-incoming.shape[1] // TILE) * TILE
    results = [jax.ShapeDtypeStruct(sums.shape, sums.dtype)]
    if turn > 0:
        results.append(jax.ShapeDtypeStruct(incoming.shape, incoming.dtype))
    return pl.pallas_call(
        functools.partial(march_kernel, turn, block, first),
        out_shape=results,
        in_specs=[ON_CHIP] * 7,
        out_specs=[ON_CHIP] * len(results),
        scratch_shapes=[pltpu.VMEM((PASS_ROWS, padded), jnp.bfloat16)],
        input_output_aliases={6: 0},
        compiler_params=pltpu.CompilerParams(vmem_limit_bytes=4 << 20),
        name="march",
    )(incoming, *held, sums)


def body(propagator, forcing, forward, damping, slowness, station_gap, freq_index):
    stations, _, width = propagator.shape
    freqs = forcing.shape[2]
    chain = lax.axis_size("stn")
    cosine, sine, slope, edge = prepare(
        station_gap, freq_index, forward, damping[None, :], slowness[None, :]
    )
    rim = from_next(edge, 1)
    half = freqs // BLOCKS
    incoming = [jnp.zeros((2 * half, width), jnp.bfloat16)] * BLOCKS
    sums = jnp.zeros((stations, width), jnp.float32)
    for turn in range(chain):
        here = chain - 1 - turn
        outgoing = []
        for block in range(BLOCKS):
            sums, *out = march(
                here, block, turn == 0, incoming[block],
                propagator, cosine, sine, forcing, slope, sums,
            )
            outgoing += [lax.ppermute(v, "stn", [(here, here - 1)]) for v in out]
        incoming = outgoing
        if turn == 0:
            slope = finish(station_gap, rim, slope, sums)
            edge, _ = lax.optimization_barrier((edge, sums))
            rim = from_next(edge, 0)
        elif turn == 1:
            slope = finish(station_gap, rim, slope, sums)
    weighting = 1.0 / (4.0 * math.sqrt(freqs * lax.axis_size("freq")))
    return summed_on_arrival(sums * weighting, "freq", 1)


def solution(mesh):
    placed = (
        P("stn", None, None),
        P("stn", None, "freq", None),
        P("stn", None, "freq", None),
        P(),
        P(),
        P("stn"),
        P("freq"),
    )
    with jax.sharding.use_abstract_mesh(mesh.abstract_mesh):
        return jax.shard_map(
            body, mesh=mesh, in_specs=placed, out_specs=P("stn", "freq"), check_vma=False
        )
```

```python
import functools
import math

import jax
import jax.numpy as jnp
from jax import lax
from jax.experimental import pallas as pl
from jax.experimental.pallas import tpu as pltpu
from jax.sharding import PartitionSpec as P

NVAR = 5
BLOCKS = 2
PASS_ROWS = 128
TILE = 256
UNITS = 2
LANES = 128

frequency_step = 0.05

ON_CHIP = pl.BlockSpec(memory_space=pltpu.VMEM)
IN_PLACE = pl.BlockSpec(memory_space=pl.ANY)
SCALARS = pl.BlockSpec(memory_space=pltpu.SMEM)


def from_next(value, parity):
    pairs = [(i, i - 1) for i in range(1, lax.axis_size("stn")) if i % 2 == parity]
    return lax.ppermute(value, "stn", pairs)


def in_blocks(value, dim, length):
    dims = value.shape
    tiles = value.reshape(*dims[:dim], length, dims[dim] // length, *dims[dim + 1 :])
    return jnp.moveaxis(tiles, dim, 0)


def summed_on_arrival(value, axis, dim):
    length = lax.axis_size(axis)
    tiles = lax.all_to_all(in_blocks(value, dim, length), axis, 0, 0, tiled=True)
    return jnp.sum(tiles, axis=0)


def prepare_kernel(
    gap_hbm, freq_index_hbm, forward_hbm, damping_hbm, slowness_hbm, forcing_hbm,
    cosine, sine, slope, edge, forcing,
    angle, wide, gap, freq_index, forward, damping, slowness, forcing_here, powers, arrived,
):
    stations, _, freqs, width = forward.shape
    padded = wide.shape[1]
    fetches = [
        pltpu.make_async_copy(source, target, arrived.at[i])
        for i, (source, target) in enumerate((
            (freq_index_hbm, freq_index), (slowness_hbm, slowness), (damping_hbm, damping),
            (gap_hbm, gap), (forward_hbm, forward), (forcing_hbm, forcing_here),
        ))
    ]
    for fetch in fetches:
        fetch.start()
    wide[...] = jnp.zeros_like(wide)
    for fetch in fetches[:4]:
        fetch.wait()
    slow = slowness[...]
    for row in range(freqs):
        frequency = frequency_step * (freq_index[row].astype(jnp.float32) + 1.0)
        angle[row : row + 1, :] = frequency * slow
    damped = jnp.exp(-damping[...])
    c1 = damped * jnp.cos(angle[...])
    s1 = damped * jnp.sin(angle[...])
    wall = width // NVAR
    place = lax.rem(lax.broadcasted_iota(jnp.int32, (freqs, padded), 1), wall)
    has_next = place != wall - 1
    has_last = place != 0
    fetches[4].wait()
    edge[...] = forward[0]
    c2 = c1 * c1 - s1 * s1
    s2 = 2.0 * (c1 * s1)
    powers[0, 0] = c1
    powers[0, 1] = s1
    powers[1, 0] = c2
    powers[1, 1] = s2
    powers[2, 0] = c2 * c1 - s2 * s1
    powers[2, 1] = c2 * s1 + s2 * c1
    fetches[5].wait()
    for station in range(stations):
        gap_here = gap[station]
        cosine[station] = powers[gap_here - 1, 0]
        sine[station] = powers[gap_here - 1, 1]
        per_gap = 1.0 / gap_here.astype(jnp.float32)
        for part in range(2):
            forcing[station, part] = forcing_here[station, part].astype(jnp.float32)
            here = forward[station, part].astype(jnp.float32)
            wide[:, :width] = here
            profile = wide[...]
            up = jnp.where(has_next, pltpu.roll(profile, padded - 1, 1), 0.0)
            down = jnp.where(has_last, pltpu.roll(profile, 1, 1), 0.0)
            normal = (0.5 * (up - down))[:, :width]
            if station + 1 < stations:
                after = forward[station + 1, part].astype(jnp.float32)
                slope[station, part] = (after - here) * per_gap + normal
            else:
                slope[station, part] = normal - here * per_gap


def prepare(gap, freq_index, forward, damping, slowness, forcing):
    stations, parts, freqs, width = forward.shape
    padded = -(-width // LANES) * LANES
    return pl.pallas_call(
        prepare_kernel,
        out_shape=(
            pltpu.VMEM((stations, freqs, width), jnp.float32),
            pltpu.VMEM((stations, freqs, width), jnp.float32),
            pltpu.VMEM((stations, parts, freqs, width), jnp.float32),
            jax.ShapeDtypeStruct((parts, freqs, width), forward.dtype),
            pltpu.VMEM((stations, parts, freqs, width), jnp.float32),
        ),
        in_specs=[IN_PLACE] * 6,
        out_specs=(ON_CHIP,) * 5,
        scratch_shapes=[
            pltpu.VMEM((freqs, width), jnp.float32),
            pltpu.VMEM((freqs, padded), jnp.float32),
            pltpu.SMEM(gap.shape, gap.dtype),
            pltpu.SMEM(freq_index.shape, freq_index.dtype),
            pltpu.VMEM(forward.shape, forward.dtype),
            pltpu.VMEM(damping.shape, damping.dtype),
            pltpu.VMEM(slowness.shape, slowness.dtype),
            pltpu.VMEM(forcing.shape, forcing.dtype),
            pltpu.VMEM((3, 2, freqs, width), jnp.float32),
            pltpu.SemaphoreType.DMA((6,)),
        ],
        cost_estimate=pl.CostEstimate(flops=16 << 30, bytes_accessed=64 << 20, transcendentals=0),
        compiler_params=pltpu.CompilerParams(vmem_limit_bytes=14 << 20),
        name="prepare",
    )(*[pltpu.with_memory_space_constraint(v, pltpu.HBM) for v in (gap, freq_index, forward, damping, slowness, forcing)])


def finish_kernel(gap, rim, slope_in, after, slope):
    del slope_in, after
    stations, parts, _, _ = slope.shape
    per_gap = 1.0 / gap[stations - 1].astype(jnp.float32)
    for part in range(parts):
        slope[stations - 1, part] += rim[part].astype(jnp.float32) * per_gap


def finish(gap, rim, slope, after):
    return pl.pallas_call(
        finish_kernel,
        out_shape=pltpu.VMEM(slope.shape, slope.dtype),
        in_specs=[SCALARS, ON_CHIP, ON_CHIP, IN_PLACE],
        out_specs=ON_CHIP,
        input_output_aliases={2: 0},
        compiler_params=pltpu.CompilerParams(vmem_limit_bytes=4 << 20),
        name="finish",
    )(gap, rim, pltpu.with_memory_space_constraint(slope, pltpu.VMEM), after)


def march_kernel(
    turn, block, first, incoming, operator, cosine, sine, forcing, slope, sums_in, *results,
):
    sums, outgoing, rows = results[0], results[1:-1], results[-1]
    stations, freqs, width = cosine.shape
    half = incoming.shape[0] // 2
    count = 2 * half
    low = block * half
    full = width // TILE
    rest = width - full * TILE
    tiles = full + 1
    groups = tiles // UNITS
    edge = width // LANES * LANES

    def settle(station, tile, mixed):
        start = tile * TILE
        size = min(TILE, width - start)
        cut = slice(start, start + size)
        real_part = forcing[station, 0, low : low + half, cut]
        imag_part = forcing[station, 1, low : low + half, cut]
        if mixed is not None:
            mixed_re, mixed_im = mixed[:half, :size], mixed[half:count, :size]
            c = cosine[station, low : low + half, cut]
            s = sine[station, low : low + half, cut]
            real_part = c * mixed_re + s * mixed_im + real_part
            imag_part = c * mixed_im - s * mixed_re + imag_part
        for place in (rows, *outgoing):
            place[:half, cut] = real_part.astype(jnp.bfloat16)
            place[half:count, cut] = imag_part.astype(jnp.bfloat16)
        product = (
            real_part * slope[station, 0, low : low + half, cut]
            + imag_part * slope[station, 1, low : low + half, cut]
        )
        total = jnp.sum(product, axis=0, keepdims=True)
        if block > 0:
            total = total + sums_in[pl.ds(station, 1), cut]
        sums[pl.ds(station, 1), cut] = total

    def run(*sums_of):
        def one(step, carried):
            station = stations - 1 - step

            def piece(depth, tile):
                deep = slice(full * TILE, width)
                if not (isinstance(depth, int) and depth == full):
                    deep = pl.ds(pl.multiple_of(depth * TILE, TILE), TILE)
                cut = slice(tile * TILE, min((tile + 1) * TILE, width))
                value = operator[station, deep, cut]
                if value.shape[1] < TILE:
                    blank = jnp.zeros((value.shape[0], TILE - rest), value.dtype)
                    value = jnp.concatenate([value, blank], axis=1)
                if value.shape[0] < TILE:
                    blank = jnp.zeros((TILE - rest, TILE), value.dtype)
                    value = jnp.concatenate([value, blank], axis=0)
                return value

            def push(depth, group):
                for unit in range(UNITS):
                    pltpu.matmul_push_rhs(piece(depth, UNITS * group + unit), group % 2, unit)

            def state_at(depth):
                return rows[:, pl.ds(pl.multiple_of(depth * TILE, TILE), TILE)]

            def accumulate(state, group):
                for unit in range(UNITS):
                    pltpu.matmul_acc_lhs(sums_of[UNITS * group + unit], state, load_staged_rhs=group % 2)

            def deepen(depth, carried):
                state = state_at(depth)
                for group in range(groups):
                    if group + 1 < groups:
                        push(depth, group + 1)
                    else:
                        push(depth + 1, 0)
                    accumulate(state, group)
                return carried

            push(0, 0)
            lax.fori_loop(0, full - 1, deepen, 0)
            deepen(full - 1, 0)
            state = rows[:, full * TILE :]
            for group in range(groups):
                if group + 1 < groups:
                    push(full, group + 1)
                accumulate(state, group)
            for tile in range(tiles):
                settle(station, tile, pltpu.matmul_pop(sums_of[tile]))
            return carried

        rows[:count, edge:] = jnp.zeros_like(rows[:count, edge:])
        if first:
            for tile in range(tiles):
                settle(stations - 1, tile, None)
            lax.fori_loop(1, stations, one, 0)
        else:
            rows[:count, :width] = incoming[...]
            lax.fori_loop(0, stations, one, 0)

    @pl.when(lax.axis_index("stn") == turn)
    def _():
        pl.run_scoped(
            run, *[pltpu.ACC(tile % UNITS)((PASS_ROWS, TILE), jnp.float32) for tile in range(tiles)]
        )


def march(turn, block, first, incoming, operator, cosine, sine, forcing, slope, sums):
    held = [pltpu.with_memory_space_constraint(v, pltpu.VMEM) for v in (operator, cosine, sine, forcing, slope)]
    padded = -(-incoming.shape[1] // TILE) * TILE
    results = [jax.ShapeDtypeStruct(sums.shape, sums.dtype)]
    if turn > 0:
        results.append(jax.ShapeDtypeStruct(incoming.shape, incoming.dtype))
    return pl.pallas_call(
        functools.partial(march_kernel, turn, block, first),
        out_shape=results,
        in_specs=[ON_CHIP] * 7,
        out_specs=[ON_CHIP] * len(results),
        scratch_shapes=[pltpu.VMEM((PASS_ROWS, padded), jnp.bfloat16)],
        input_output_aliases={6: 0},
        compiler_params=pltpu.CompilerParams(vmem_limit_bytes=4 << 20),
        name="march",
    )(incoming, *held, sums)


def body(propagator, forcing, forward, damping, slowness, station_gap, freq_index):
    stations, _, width = propagator.shape
    freqs = forcing.shape[2]
    chain = lax.axis_size("stn")
    cosine, sine, slope, edge, forcing = prepare(
        station_gap, freq_index, forward, damping[None, :], slowness[None, :], forcing
    )
    rim = from_next(edge, 1)
    half = freqs // BLOCKS
    incoming = [jnp.zeros((2 * half, width), jnp.bfloat16)] * BLOCKS
    sums = jnp.zeros((stations, width), jnp.float32)
    for turn in range(chain):
        here = chain - 1 - turn
        outgoing = []
        for block in range(BLOCKS):
            sums, *out = march(
                here, block, turn == 0, incoming[block],
                propagator, cosine, sine, forcing, slope, sums,
            )
            outgoing += [lax.ppermute(v, "stn", [(here, here - 1)]) for v in out]
        incoming = outgoing
        if turn == 0:
            slope = finish(station_gap, rim, slope, sums)
            edge, _ = lax.optimization_barrier((edge, sums))
            rim = from_next(edge, 0)
        elif turn == 1:
            slope = finish(station_gap, rim, slope, sums)
    weighting = 1.0 / (4.0 * math.sqrt(freqs * lax.axis_size("freq")))
    return summed_on_arrival(sums * weighting, "freq", 1)


def solution(mesh):
    placed = (
        P("stn", None, None),
        P("stn", None, "freq", None),
        P("stn", None, "freq", None),
        P(),
        P(),
        P("stn"),
        P("freq"),
    )
    with jax.sharding.use_abstract_mesh(mesh.abstract_mesh):
        return jax.shard_map(
            body, mesh=mesh, in_specs=placed, out_specs=P("stn", "freq"), check_vma=False
        )
```

```python
import functools
import math

import jax
import jax.numpy as jnp
from jax import lax
from jax.experimental import pallas as pl
from jax.experimental.pallas import tpu as pltpu
from jax.sharding import PartitionSpec as P

NVAR = 5
BLOCKS = 2
PASS_ROWS = 128
TILE = 256
UNITS = 2
LANES = 128

frequency_step = 0.05

ON_CHIP = pl.BlockSpec(memory_space=pltpu.VMEM)
IN_PLACE = pl.BlockSpec(memory_space=pl.ANY)
SCALARS = pl.BlockSpec(memory_space=pltpu.SMEM)


def from_next(value, parity):
    pairs = [(i, i - 1) for i in range(1, lax.axis_size("stn")) if i % 2 == parity]
    return lax.ppermute(value, "stn", pairs)


def in_blocks(value, dim, length):
    dims = value.shape
    tiles = value.reshape(*dims[:dim], length, dims[dim] // length, *dims[dim + 1 :])
    return jnp.moveaxis(tiles, dim, 0)


def summed_on_arrival(value, axis, dim):
    length = lax.axis_size(axis)
    tiles = lax.all_to_all(in_blocks(value, dim, length), axis, 0, 0, tiled=True)
    return jnp.sum(tiles, axis=0)


def prepare_kernel(
    gap_hbm, freq_index_hbm, forward_hbm, damping_hbm, slowness_hbm, forcing_hbm,
    cosine, sine, slope, edge, forcing,
    angle, wide, gap, freq_index, forward, damping, slowness, forcing_here, powers, arrived,
):
    stations, _, freqs, width = forward.shape
    padded = wide.shape[1]
    fetches = [
        pltpu.make_async_copy(source, target, arrived.at[i])
        for i, (source, target) in enumerate((
            (freq_index_hbm, freq_index), (slowness_hbm, slowness), (damping_hbm, damping),
            (gap_hbm, gap), (forward_hbm, forward), (forcing_hbm, forcing_here),
        ))
    ]
    for fetch in fetches:
        fetch.start()
    wide[...] = jnp.zeros_like(wide)
    for fetch in fetches[:4]:
        fetch.wait()
    slow = slowness[...]
    for row in range(freqs):
        frequency = frequency_step * (freq_index[row].astype(jnp.float32) + 1.0)
        angle[row : row + 1, :] = frequency * slow
    damped = jnp.exp(-damping[...])
    c1 = damped * jnp.cos(angle[...])
    s1 = damped * jnp.sin(angle[...])
    wall = width // NVAR
    place = lax.rem(lax.broadcasted_iota(jnp.int32, (freqs, padded), 1), wall)
    has_next = place != wall - 1
    has_last = place != 0
    fetches[4].wait()
    edge[...] = forward[0]
    c2 = c1 * c1 - s1 * s1
    s2 = 2.0 * (c1 * s1)
    powers[0, 0] = c1
    powers[0, 1] = s1
    powers[1, 0] = c2
    powers[1, 1] = s2
    powers[2, 0] = c2 * c1 - s2 * s1
    powers[2, 1] = c2 * s1 + s2 * c1
    fetches[5].wait()
    for station in range(stations):
        gap_here = gap[station]
        cosine[station] = powers[gap_here - 1, 0]
        sine[station] = powers[gap_here - 1, 1]
        per_gap = 1.0 / gap_here.astype(jnp.float32)
        for part in range(2):
            forcing[station, part] = forcing_here[station, part].astype(jnp.float32)
            here = forward[station, part].astype(jnp.float32)
            wide[:, :width] = here
            profile = wide[...]
            up = jnp.where(has_next, pltpu.roll(profile, padded - 1, 1), 0.0)
            down = jnp.where(has_last, pltpu.roll(profile, 1, 1), 0.0)
            normal = (0.5 * (up - down))[:, :width]
            if station + 1 < stations:
                after = forward[station + 1, part].astype(jnp.float32)
                slope[station, part] = (after - here) * per_gap + normal
            else:
                slope[station, part] = normal - here * per_gap


def prepare(gap, freq_index, forward, damping, slowness, forcing):
    stations, parts, freqs, width = forward.shape
    padded = -(-width // LANES) * LANES
    return pl.pallas_call(
        prepare_kernel,
        out_shape=(
            pltpu.VMEM((stations, freqs, width), jnp.float32),
            pltpu.VMEM((stations, freqs, width), jnp.float32),
            pltpu.VMEM((stations, parts, freqs, width), jnp.float32),
            jax.ShapeDtypeStruct((parts, freqs, width), forward.dtype),
            pltpu.VMEM((stations, parts, freqs, width), jnp.float32),
        ),
        in_specs=[IN_PLACE] * 6,
        out_specs=(ON_CHIP,) * 5,
        scratch_shapes=[
            pltpu.VMEM((freqs, width), jnp.float32),
            pltpu.VMEM((freqs, padded), jnp.float32),
            pltpu.SMEM(gap.shape, gap.dtype),
            pltpu.SMEM(freq_index.shape, freq_index.dtype),
            pltpu.VMEM(forward.shape, forward.dtype),
            pltpu.VMEM(damping.shape, damping.dtype),
            pltpu.VMEM(slowness.shape, slowness.dtype),
            pltpu.VMEM(forcing.shape, forcing.dtype),
            pltpu.VMEM((3, 2, freqs, width), jnp.float32),
            pltpu.SemaphoreType.DMA((6,)),
        ],
        cost_estimate=pl.CostEstimate(flops=16 << 30, bytes_accessed=64 << 20, transcendentals=0),
        compiler_params=pltpu.CompilerParams(vmem_limit_bytes=14 << 20),
        name="prepare",
    )(*[pltpu.with_memory_space_constraint(v, pltpu.HBM) for v in (gap, freq_index, forward, damping, slowness, forcing)])


def finish_kernel(gap, rim, slope_in, after, slope):
    del slope_in, after
    stations, parts, _, _ = slope.shape
    per_gap = 1.0 / gap[stations - 1].astype(jnp.float32)
    for part in range(parts):
        slope[stations - 1, part] += rim[part].astype(jnp.float32) * per_gap


def finish(gap, rim, slope, after):
    return pl.pallas_call(
        finish_kernel,
        out_shape=pltpu.VMEM(slope.shape, slope.dtype),
        in_specs=[SCALARS, ON_CHIP, ON_CHIP, IN_PLACE],
        out_specs=ON_CHIP,
        input_output_aliases={2: 0},
        compiler_params=pltpu.CompilerParams(vmem_limit_bytes=4 << 20),
        name="finish",
    )(gap, rim, pltpu.with_memory_space_constraint(slope, pltpu.VMEM), after)


def march_kernel(
    turn, block, first, incoming, operator, cosine, sine, forcing, slope, sums_in, *results,
):
    sums, rows = results
    repeat = PASS_ROWS // incoming.shape[0]
    stations, freqs, width = cosine.shape
    half = rows.shape[0] // 2
    count = 2 * half
    low = block * half
    full = width // TILE
    rest = width - full * TILE
    tiles = full + 1
    groups = tiles // UNITS
    del incoming

    def settle(station, tile, mixed):
        start = tile * TILE
        size = min(TILE, width - start)
        cut = slice(start, start + size)
        real_part = forcing[station, 0, low : low + half, cut]
        imag_part = forcing[station, 1, low : low + half, cut]
        if mixed is not None:
            mixed_re, mixed_im = mixed[:half, :size], mixed[half:count, :size]
            c = cosine[station, low : low + half, cut]
            s = sine[station, low : low + half, cut]
            real_part = c * mixed_re + s * mixed_im + real_part
            imag_part = c * mixed_im - s * mixed_re + imag_part
        rows[:half, cut] = real_part.astype(jnp.bfloat16)
        rows[half:, cut] = imag_part.astype(jnp.bfloat16)
        product = (
            real_part * slope[station, 0, low : low + half, cut]
            + imag_part * slope[station, 1, low : low + half, cut]
        )
        total = jnp.sum(product, axis=0, keepdims=True)
        if block > 0:
            total = total + sums_in[pl.ds(station, 1), cut]
        sums[pl.ds(station, 1), cut] = total

    def run(*sums_of):
        def one(step, carried):
            station = stations - 1 - step

            def piece(depth, tile):
                deep = slice(full * TILE, width)
                if not (isinstance(depth, int) and depth == full):
                    deep = pl.ds(pl.multiple_of(depth * TILE, TILE), TILE)
                cut = slice(tile * TILE, min((tile + 1) * TILE, width))
                value = operator[station, deep, cut]
                if value.shape[1] < TILE:
                    blank = jnp.zeros((value.shape[0], TILE - rest), value.dtype)
                    value = jnp.concatenate([value, blank], axis=1)
                if value.shape[0] < TILE:
                    blank = jnp.zeros((TILE - rest, TILE), value.dtype)
                    value = jnp.concatenate([value, blank], axis=0)
                return value

            def push(depth, group):
                for unit in range(UNITS):
                    pltpu.matmul_push_rhs(piece(depth, UNITS * group + unit), group % 2, unit)

            def state_at(depth):
                held = rows[:, pl.ds(pl.multiple_of(depth * TILE, TILE), TILE)]
                return jnp.concatenate([held] * repeat, axis=0)

            def accumulate(state, group):
                for unit in range(UNITS):
                    pltpu.matmul_acc_lhs(sums_of[UNITS * group + unit], state, load_staged_rhs=group % 2)

            def deepen(depth, carried):
                state = state_at(depth)
                for group in range(groups):
                    if group + 1 < groups:
                        push(depth, group + 1)
                    else:
                        push(depth + 1, 0)
                    accumulate(state, group)
                return carried

            push(0, 0)
            lax.fori_loop(0, full - 1, deepen, 0)
            deepen(full - 1, 0)
            state = state_at(full)
            for group in range(groups):
                if group + 1 < groups:
                    push(full, group + 1)
                accumulate(state, group)
            for tile in range(tiles):
                settle(station, tile, pltpu.matmul_pop(sums_of[tile]))
            return carried

        if first:
            for tile in range(tiles):
                settle(stations - 1, tile, None)
            lax.fori_loop(1, stations, one, 0)
        else:
            lax.fori_loop(0, stations, one, 0)

    @pl.when(lax.axis_index("stn") == turn)
    def _():
        pl.run_scoped(
            run, *[pltpu.ACC(tile % UNITS)((PASS_ROWS, TILE), jnp.float32) for tile in range(tiles)]
        )


def march(turn, block, first, incoming, operator, cosine, sine, forcing, slope, sums):
    held = [pltpu.with_memory_space_constraint(v, pltpu.VMEM) for v in (operator, cosine, sine, forcing, slope)]
    return pl.pallas_call(
        functools.partial(march_kernel, turn, block, first),
        out_shape=[jax.ShapeDtypeStruct(v.shape, v.dtype) for v in (sums, incoming)],
        in_specs=[ON_CHIP] * 7,
        out_specs=[ON_CHIP] * 2,
        input_output_aliases={6: 0, 0: 1},
        compiler_params=pltpu.CompilerParams(vmem_limit_bytes=4 << 20),
        name="march",
    )(pltpu.with_memory_space_constraint(incoming, pltpu.VMEM), *held, sums)


def body(propagator, forcing, forward, damping, slowness, station_gap, freq_index):
    stations, _, width = propagator.shape
    freqs = forcing.shape[2]
    chain = lax.axis_size("stn")
    cosine, sine, slope, edge, forcing = prepare(
        station_gap, freq_index, forward, damping[None, :], slowness[None, :], forcing
    )
    rim = from_next(edge, 1)
    half = freqs // BLOCKS
    padded = -(-width // TILE) * TILE
    incoming = [jnp.zeros((2 * half, padded), jnp.bfloat16)] * BLOCKS
    sums = jnp.zeros((stations, width), jnp.float32)
    for turn in range(chain):
        here = chain - 1 - turn
        outgoing = []
        for block in range(BLOCKS):
            sums, out = march(
                here, block, turn == 0, incoming[block],
                propagator, cosine, sine, forcing, slope, sums,
            )
            if here > 0:
                outgoing.append(lax.ppermute(out, "stn", [(here, here - 1)]))
        incoming = outgoing
        if turn == 0:
            slope = finish(station_gap, rim, slope, sums)
            edge, _ = lax.optimization_barrier((edge, sums))
            rim = from_next(edge, 0)
        elif turn == 1:
            slope = finish(station_gap, rim, slope, sums)
    weighting = 1.0 / (4.0 * math.sqrt(freqs * lax.axis_size("freq")))
    return summed_on_arrival(sums * weighting, "freq", 1)


def solution(mesh):
    placed = (
        P("stn", None, None),
        P("stn", None, "freq", None),
        P("stn", None, "freq", None),
        P(),
        P(),
        P("stn"),
        P("freq"),
    )
    with jax.sharding.use_abstract_mesh(mesh.abstract_mesh):
        return jax.shard_map(
            body, mesh=mesh, in_specs=placed, out_specs=P("stn", "freq"), check_vma=False
        )
```

```python
import functools
import math

import jax
import jax.numpy as jnp
from jax import lax
from jax.experimental import pallas as pl
from jax.experimental.pallas import tpu as pltpu
from jax.sharding import PartitionSpec as P

NVAR = 5
BLOCKS = 2
PASS_ROWS = 128
TILE = 256
UNITS = 2
LANES = 128

frequency_step = 0.05

ON_CHIP = pl.BlockSpec(memory_space=pltpu.VMEM)
IN_PLACE = pl.BlockSpec(memory_space=pl.ANY)
SCALARS = pl.BlockSpec(memory_space=pltpu.SMEM)


def from_next(value, parity):
    pairs = [(i, i - 1) for i in range(1, lax.axis_size("stn")) if i % 2 == parity]
    return lax.ppermute(value, "stn", pairs)


def in_blocks(value, dim, length):
    dims = value.shape
    tiles = value.reshape(*dims[:dim], length, dims[dim] // length, *dims[dim + 1 :])
    return jnp.moveaxis(tiles, dim, 0)


def summed_on_arrival(value, axis, dim):
    length = lax.axis_size(axis)
    tiles = lax.all_to_all(in_blocks(value, dim, length), axis, 0, 0, tiled=True)
    return jnp.sum(tiles, axis=0)


def prepare_kernel(
    gap_hbm, freq_index_hbm, forward_hbm, damping_hbm, slowness_hbm, forcing_hbm,
    cosine, sine, slope, edge, forcing,
    angle, wide, gap, freq_index, forward, damping, slowness, forcing_here, powers, arrived,
):
    stations, _, freqs, width = forward.shape
    padded = wide.shape[1]
    fetches = [
        pltpu.make_async_copy(source, target, arrived.at[i])
        for i, (source, target) in enumerate((
            (freq_index_hbm, freq_index), (slowness_hbm, slowness), (damping_hbm, damping),
            (gap_hbm, gap), (forward_hbm, forward), (forcing_hbm, forcing_here),
        ))
    ]
    for fetch in fetches:
        fetch.start()
    wide[...] = jnp.zeros_like(wide)
    for fetch in fetches[:4]:
        fetch.wait()
    slow = slowness[...]
    for row in range(freqs):
        frequency = frequency_step * (freq_index[row].astype(jnp.float32) + 1.0)
        angle[row : row + 1, :] = frequency * slow
    damped = jnp.exp(-damping[...])
    c1 = damped * jnp.cos(angle[...])
    s1 = damped * jnp.sin(angle[...])
    wall = width // NVAR
    place = lax.rem(lax.broadcasted_iota(jnp.int32, (freqs, padded), 1), wall)
    has_next = place != wall - 1
    has_last = place != 0
    fetches[4].wait()
    edge[...] = forward[0]
    c2 = c1 * c1 - s1 * s1
    s2 = 2.0 * (c1 * s1)
    powers[0, 0] = c1
    powers[0, 1] = s1
    powers[1, 0] = c2
    powers[1, 1] = s2
    powers[2, 0] = c2 * c1 - s2 * s1
    powers[2, 1] = c2 * s1 + s2 * c1
    fetches[5].wait()
    for station in range(stations):
        gap_here = gap[station]
        cosine[station] = powers[gap_here - 1, 0]
        sine[station] = powers[gap_here - 1, 1]
        per_gap = 1.0 / gap_here.astype(jnp.float32)
        for part in range(2):
            forcing[station, part] = forcing_here[station, part].astype(jnp.float32)
            here = forward[station, part].astype(jnp.float32)
            wide[:, :width] = here
            profile = wide[...]
            up = jnp.where(has_next, pltpu.roll(profile, padded - 1, 1), 0.0)
            down = jnp.where(has_last, pltpu.roll(profile, 1, 1), 0.0)
            normal = (0.5 * (up - down))[:, :width]
            if station + 1 < stations:
                after = forward[station + 1, part].astype(jnp.float32)
                slope[station, part] = (after - here) * per_gap + normal
            else:
                slope[station, part] = normal - here * per_gap


def prepare(gap, freq_index, forward, damping, slowness, forcing):
    stations, parts, freqs, width = forward.shape
    padded = -(-width // LANES) * LANES
    return pl.pallas_call(
        prepare_kernel,
        out_shape=(
            pltpu.VMEM((stations, freqs, width), jnp.float32),
            pltpu.VMEM((stations, freqs, width), jnp.float32),
            pltpu.VMEM((stations, parts, freqs, width), jnp.float32),
            jax.ShapeDtypeStruct((parts, freqs, width), forward.dtype),
            pltpu.VMEM((stations, parts, freqs, width), jnp.float32),
        ),
        in_specs=[IN_PLACE] * 6,
        out_specs=(ON_CHIP,) * 5,
        scratch_shapes=[
            pltpu.VMEM((freqs, width), jnp.float32),
            pltpu.VMEM((freqs, padded), jnp.float32),
            pltpu.SMEM(gap.shape, gap.dtype),
            pltpu.SMEM(freq_index.shape, freq_index.dtype),
            pltpu.VMEM(forward.shape, forward.dtype),
            pltpu.VMEM(damping.shape, damping.dtype),
            pltpu.VMEM(slowness.shape, slowness.dtype),
            pltpu.VMEM(forcing.shape, forcing.dtype),
            pltpu.VMEM((3, 2, freqs, width), jnp.float32),
            pltpu.SemaphoreType.DMA((6,)),
        ],
        cost_estimate=pl.CostEstimate(flops=16 << 30, bytes_accessed=64 << 20, transcendentals=0),
        compiler_params=pltpu.CompilerParams(vmem_limit_bytes=14 << 20),
        name="prepare",
    )(*[pltpu.with_memory_space_constraint(v, pltpu.HBM) for v in (gap, freq_index, forward, damping, slowness, forcing)])


def finish_kernel(gap, rim, slope_in, after, slope):
    del slope_in, after
    stations, parts, _, _ = slope.shape
    per_gap = 1.0 / gap[stations - 1].astype(jnp.float32)
    for part in range(parts):
        slope[stations - 1, part] += rim[part].astype(jnp.float32) * per_gap


def finish(gap, rim, slope, after):
    return pl.pallas_call(
        finish_kernel,
        out_shape=pltpu.VMEM(slope.shape, slope.dtype),
        in_specs=[SCALARS, ON_CHIP, ON_CHIP, IN_PLACE],
        out_specs=ON_CHIP,
        input_output_aliases={2: 0},
        compiler_params=pltpu.CompilerParams(vmem_limit_bytes=4 << 20),
        name="finish",
    )(gap, rim, pltpu.with_memory_space_constraint(slope, pltpu.VMEM), after)


def march_kernel(
    turn, block, first, incoming, operator, cosine, sine, forcing, slope, sums_in, *results,
):
    sums, rows = results
    repeat = PASS_ROWS // incoming.shape[0]
    stations, freqs, width = cosine.shape
    half = rows.shape[0] // 2
    count = 2 * half
    low = block * half
    full = width // TILE
    rest = width - full * TILE
    tiles = full + 1
    groups = tiles // UNITS
    del incoming

    def settle(station, tile, mixed):
        start = tile * TILE
        size = min(TILE, width - start)
        cut = slice(start, start + size)
        real_part = forcing[station, 0, low : low + half, cut]
        imag_part = forcing[station, 1, low : low + half, cut]
        if mixed is not None:
            mixed_re, mixed_im = mixed[:half, :size], mixed[half:count, :size]
            c = cosine[station, low : low + half, cut]
            s = sine[station, low : low + half, cut]
            real_part = c * mixed_re + s * mixed_im + real_part
            imag_part = c * mixed_im - s * mixed_re + imag_part
        rows[:half, cut] = real_part.astype(jnp.bfloat16)
        rows[half:, cut] = imag_part.astype(jnp.bfloat16)
        product = (
            real_part * slope[station, 0, low : low + half, cut]
            + imag_part * slope[station, 1, low : low + half, cut]
        )
        total = jnp.sum(product, axis=0, keepdims=True)
        if block > 0:
            total = total + sums_in[pl.ds(station, 1), cut]
        sums[pl.ds(station, 1), cut] = total

    def run(*sums_of):
        def one(step, carried):
            station = stations - 1 - step

            def piece(depth, tile):
                deep = slice(full * TILE, width)
                if not (isinstance(depth, int) and depth == full):
                    deep = pl.ds(pl.multiple_of(depth * TILE, TILE), TILE)
                cut = slice(tile * TILE, min((tile + 1) * TILE, width))
                value = operator[station, deep, cut]
                if value.shape[1] < TILE:
                    blank = jnp.zeros((value.shape[0], TILE - rest), value.dtype)
                    value = jnp.concatenate([value, blank], axis=1)
                if value.shape[0] < TILE:
                    blank = jnp.zeros((TILE - rest, TILE), value.dtype)
                    value = jnp.concatenate([value, blank], axis=0)
                return value

            def push(depth, group):
                for unit in range(UNITS):
                    pltpu.matmul_push_rhs(piece(depth, UNITS * group + unit), group % 2, unit)

            def state_at(depth):
                held = rows[:, pl.ds(pl.multiple_of(depth * TILE, TILE), TILE)]
                return jnp.concatenate([held] * repeat, axis=0)

            def accumulate(state, group):
                for unit in range(UNITS):
                    pltpu.matmul_acc_lhs(sums_of[UNITS * group + unit], state, load_staged_rhs=group % 2)

            def deepen(depth, carried):
                state = state_at(depth)
                for group in range(groups):
                    if group + 1 < groups:
                        push(depth, group + 1)
                    else:
                        push(depth + 1, 0)
                    accumulate(state, group)
                return carried

            push(0, 0)
            lax.fori_loop(0, full - 1, deepen, 0)
            states = [state_at(full - 1), state_at(full)]
            order = [(late, group) for group in range(groups) for late in range(2)]

            def push_late(turn):
                late, group = order[turn]
                for unit in range(UNITS):
                    pltpu.matmul_push_rhs(piece(full - 1 + late, UNITS * group + unit), turn % 2, unit)

            for turn, (late, group) in enumerate(order):
                if turn + 1 < len(order):
                    push_late(turn + 1)
                for unit in range(UNITS):
                    pltpu.matmul_acc_lhs(sums_of[UNITS * group + unit], states[late], load_staged_rhs=turn % 2)
                if late == 0 and group > 0:
                    for tile in range(UNITS * (group - 1), UNITS * group):
                        settle(station, tile, pltpu.matmul_pop(sums_of[tile]))
            for tile in range(UNITS * (groups - 1), tiles):
                settle(station, tile, pltpu.matmul_pop(sums_of[tile]))
            return carried

        if first:
            for tile in range(tiles):
                settle(stations - 1, tile, None)
            lax.fori_loop(1, stations, one, 0)
        else:
            lax.fori_loop(0, stations, one, 0)

    @pl.when(lax.axis_index("stn") == turn)
    def _():
        pl.run_scoped(
            run, *[pltpu.ACC(tile % UNITS)((PASS_ROWS, TILE), jnp.float32) for tile in range(tiles)]
        )


def march(turn, block, first, incoming, operator, cosine, sine, forcing, slope, sums):
    held = [pltpu.with_memory_space_constraint(v, pltpu.VMEM) for v in (operator, cosine, sine, forcing, slope)]
    return pl.pallas_call(
        functools.partial(march_kernel, turn, block, first),
        out_shape=[jax.ShapeDtypeStruct(v.shape, v.dtype) for v in (sums, incoming)],
        in_specs=[ON_CHIP] * 7,
        out_specs=[ON_CHIP] * 2,
        input_output_aliases={6: 0, 0: 1},
        compiler_params=pltpu.CompilerParams(vmem_limit_bytes=4 << 20),
        name="march",
    )(pltpu.with_memory_space_constraint(incoming, pltpu.VMEM), *held, sums)


def body(propagator, forcing, forward, damping, slowness, station_gap, freq_index):
    stations, _, width = propagator.shape
    freqs = forcing.shape[2]
    chain = lax.axis_size("stn")
    cosine, sine, slope, edge, forcing = prepare(
        station_gap, freq_index, forward, damping[None, :], slowness[None, :], forcing
    )
    rim = from_next(edge, 1)
    half = freqs // BLOCKS
    padded = -(-width // TILE) * TILE
    incoming = [jnp.zeros((2 * half, padded), jnp.bfloat16)] * BLOCKS
    sums = jnp.zeros((stations, width), jnp.float32)
    for turn in range(chain):
        here = chain - 1 - turn
        outgoing = []
        for block in range(BLOCKS):
            sums, out = march(
                here, block, turn == 0, incoming[block],
                propagator, cosine, sine, forcing, slope, sums,
            )
            if here > 0:
                outgoing.append(lax.ppermute(out, "stn", [(here, here - 1)]))
        incoming = outgoing
        if turn == 0:
            slope = finish(station_gap, rim, slope, sums)
            edge, _ = lax.optimization_barrier((edge, sums))
            rim = from_next(edge, 0)
        elif turn == 1:
            slope = finish(station_gap, rim, slope, sums)
    weighting = 1.0 / (4.0 * math.sqrt(freqs * lax.axis_size("freq")))
    return summed_on_arrival(sums * weighting, "freq", 1)


def solution(mesh):
    placed = (
        P("stn", None, None),
        P("stn", None, "freq", None),
        P("stn", None, "freq", None),
        P(),
        P(),
        P("stn"),
        P("freq"),
    )
    with jax.sharding.use_abstract_mesh(mesh.abstract_mesh):
        return jax.shard_map(
            body, mesh=mesh, in_specs=placed, out_specs=P("stn", "freq"), check_vma=False
        )
```

```python
import functools
import math

import jax
import jax.numpy as jnp
from jax import lax
from jax.experimental import pallas as pl
from jax.experimental.pallas import tpu as pltpu
from jax.sharding import PartitionSpec as P

NVAR = 5
BLOCKS = 2
PASS_ROWS = 128
TILE = 256
UNITS = 2
LANES = 128

frequency_step = 0.05

ON_CHIP = pl.BlockSpec(memory_space=pltpu.VMEM)
IN_PLACE = pl.BlockSpec(memory_space=pl.ANY)
SCALARS = pl.BlockSpec(memory_space=pltpu.SMEM)


def from_next(value, parity):
    pairs = [(i, i - 1) for i in range(1, lax.axis_size("stn")) if i % 2 == parity]
    return lax.ppermute(value, "stn", pairs)


def in_blocks(value, dim, length):
    dims = value.shape
    tiles = value.reshape(*dims[:dim], length, dims[dim] // length, *dims[dim + 1 :])
    return jnp.moveaxis(tiles, dim, 0)


def summed_on_arrival(value, axis, dim):
    length = lax.axis_size(axis)
    tiles = lax.all_to_all(in_blocks(value, dim, length), axis, 0, 0, tiled=True)
    return jnp.sum(tiles, axis=0)


def prepare_kernel(
    gap_hbm, freq_index_hbm, forward_hbm, damping_hbm, slowness_hbm, forcing_hbm,
    cosine, sine, slope, edge, forcing,
    angle, wide, gap, freq_index, forward, damping, slowness, forcing_here, powers, arrived,
):
    stations, _, freqs, width = forward.shape
    padded = wide.shape[1]
    fetches = [
        pltpu.make_async_copy(source, target, arrived.at[i])
        for i, (source, target) in enumerate((
            (freq_index_hbm, freq_index), (slowness_hbm, slowness), (damping_hbm, damping),
            (gap_hbm, gap), (forward_hbm, forward), (forcing_hbm, forcing_here),
        ))
    ]
    for fetch in fetches:
        fetch.start()
    wide[...] = jnp.zeros_like(wide)
    for fetch in fetches[:4]:
        fetch.wait()
    slow = slowness[...]
    for row in range(freqs):
        frequency = frequency_step * (freq_index[row].astype(jnp.float32) + 1.0)
        angle[row : row + 1, :] = frequency * slow
    damped = jnp.exp(-damping[...])
    c1 = damped * jnp.cos(angle[...])
    s1 = damped * jnp.sin(angle[...])
    wall = width // NVAR
    place = lax.rem(lax.broadcasted_iota(jnp.int32, (freqs, padded), 1), wall)
    has_next = place != wall - 1
    has_last = place != 0
    fetches[4].wait()
    edge[...] = forward[0]
    c2 = c1 * c1 - s1 * s1
    s2 = 2.0 * (c1 * s1)
    powers[0, 0] = c1
    powers[0, 1] = s1
    powers[1, 0] = c2
    powers[1, 1] = s2
    powers[2, 0] = c2 * c1 - s2 * s1
    powers[2, 1] = c2 * s1 + s2 * c1
    fetches[5].wait()
    for station in range(stations):
        gap_here = gap[station]
        cosine[station] = powers[gap_here - 1, 0]
        sine[station] = powers[gap_here - 1, 1]
        per_gap = 1.0 / gap_here.astype(jnp.float32)
        for part in range(2):
            forcing[station, part] = forcing_here[station, part].astype(jnp.float32)
            here = forward[station, part].astype(jnp.float32)
            wide[:, :width] = here
            profile = wide[...]
            up = jnp.where(has_next, pltpu.roll(profile, padded - 1, 1), 0.0)
            down = jnp.where(has_last, pltpu.roll(profile, 1, 1), 0.0)
            normal = (0.5 * (up - down))[:, :width]
            if station + 1 < stations:
                after = forward[station + 1, part].astype(jnp.float32)
                slope[station, part] = (after - here) * per_gap + normal
            else:
                slope[station, part] = normal - here * per_gap


def prepare(gap, freq_index, forward, damping, slowness, forcing):
    stations, parts, freqs, width = forward.shape
    padded = -(-width // LANES) * LANES
    return pl.pallas_call(
        prepare_kernel,
        out_shape=(
            pltpu.VMEM((stations, freqs, width), jnp.float32),
            pltpu.VMEM((stations, freqs, width), jnp.float32),
            pltpu.VMEM((stations, parts, freqs, width), jnp.float32),
            jax.ShapeDtypeStruct((parts, freqs, width), forward.dtype),
            pltpu.VMEM((stations, parts, freqs, width), jnp.float32),
        ),
        in_specs=[IN_PLACE] * 6,
        out_specs=(ON_CHIP,) * 5,
        scratch_shapes=[
            pltpu.VMEM((freqs, width), jnp.float32),
            pltpu.VMEM((freqs, padded), jnp.float32),
            pltpu.SMEM(gap.shape, gap.dtype),
            pltpu.SMEM(freq_index.shape, freq_index.dtype),
            pltpu.VMEM(forward.shape, forward.dtype),
            pltpu.VMEM(damping.shape, damping.dtype),
            pltpu.VMEM(slowness.shape, slowness.dtype),
            pltpu.VMEM(forcing.shape, forcing.dtype),
            pltpu.VMEM((3, 2, freqs, width), jnp.float32),
            pltpu.SemaphoreType.DMA((6,)),
        ],
        cost_estimate=pl.CostEstimate(flops=16 << 30, bytes_accessed=64 << 20, transcendentals=0),
        compiler_params=pltpu.CompilerParams(vmem_limit_bytes=14 << 20),
        name="prepare",
    )(*[pltpu.with_memory_space_constraint(v, pltpu.HBM) for v in (gap, freq_index, forward, damping, slowness, forcing)])


def finish_kernel(gap, rim, slope_in, after, slope):
    del slope_in, after
    stations, parts, _, _ = slope.shape
    per_gap = 1.0 / gap[stations - 1].astype(jnp.float32)
    for part in range(parts):
        slope[stations - 1, part] += rim[part].astype(jnp.float32) * per_gap


def finish(gap, rim, slope, after):
    return pl.pallas_call(
        finish_kernel,
        out_shape=pltpu.VMEM(slope.shape, slope.dtype),
        in_specs=[SCALARS, ON_CHIP, ON_CHIP, IN_PLACE],
        out_specs=ON_CHIP,
        input_output_aliases={2: 0},
        compiler_params=pltpu.CompilerParams(vmem_limit_bytes=4 << 20),
        name="finish",
    )(gap, rim, pltpu.with_memory_space_constraint(slope, pltpu.VMEM), after)


def march_kernel(
    turn, block, first, incoming, operator, cosine, sine, forcing, slope, sums_in, *results,
):
    sums, rows = results
    repeat = PASS_ROWS // incoming.shape[0]
    stations, freqs, width = cosine.shape
    half = rows.shape[0] // 2
    count = 2 * half
    low = block * half
    full = width // TILE
    rest = width - full * TILE
    tiles = full + 1
    groups = tiles // UNITS
    del incoming

    def settle(station, tile, mixed):
        start = tile * TILE
        size = min(TILE, width - start)
        cut = slice(start, start + size)
        real_part = forcing[station, 0, low : low + half, cut]
        imag_part = forcing[station, 1, low : low + half, cut]
        if mixed is not None:
            mixed_re, mixed_im = mixed[:half, :size], mixed[half:count, :size]
            c = cosine[station, low : low + half, cut]
            s = sine[station, low : low + half, cut]
            real_part = c * mixed_re + s * mixed_im + real_part
            imag_part = c * mixed_im - s * mixed_re + imag_part
        rows[:half, cut] = real_part.astype(jnp.bfloat16)
        rows[half:, cut] = imag_part.astype(jnp.bfloat16)
        product = (
            real_part * slope[station, 0, low : low + half, cut]
            + imag_part * slope[station, 1, low : low + half, cut]
        )
        total = jnp.sum(product, axis=0, keepdims=True)
        if block > 0:
            total = total + sums_in[pl.ds(station, 1), cut]
        sums[pl.ds(station, 1), cut] = total

    def run(*sums_of):
        def one(step, carried):
            station = stations - 1 - step

            def piece(depth, tile):
                deep = slice(full * TILE, width)
                if not (isinstance(depth, int) and depth == full):
                    deep = pl.ds(pl.multiple_of(depth * TILE, TILE), TILE)
                cut = slice(tile * TILE, min((tile + 1) * TILE, width))
                value = operator[station, deep, cut]
                if value.shape[1] < TILE:
                    blank = jnp.zeros((value.shape[0], TILE - rest), value.dtype)
                    value = jnp.concatenate([value, blank], axis=1)
                if value.shape[0] < TILE:
                    blank = jnp.zeros((TILE - rest, TILE), value.dtype)
                    value = jnp.concatenate([value, blank], axis=0)
                return value

            def push(depth, group):
                for unit in range(UNITS):
                    pltpu.matmul_push_rhs(piece(depth, UNITS * group + unit), group % 2, unit)

            def state_at(depth):
                held = rows[:, pl.ds(pl.multiple_of(depth * TILE, TILE), TILE)]
                return jnp.concatenate([held] * repeat, axis=0)

            def accumulate(state, group):
                for unit in range(UNITS):
                    pltpu.matmul_acc_lhs(sums_of[UNITS * group + unit], state, load_staged_rhs=group % 2)

            def deepen(depth, carried):
                state = state_at(depth)
                for group in range(groups):
                    if group + 1 < groups:
                        push(depth, group + 1)
                    else:
                        push(depth + 1, 0)
                    accumulate(state, group)
                return carried

            push(0, 0)
            def deepen_twice(step, carried):
                return deepen(2 * step + 1, deepen(2 * step, carried))

            if block == 0:
                lax.fori_loop(0, (full - 1) // 2, deepen_twice, 0)
                if (full - 1) % 2:
                    deepen(full - 2, 0)
            else:
                lax.fori_loop(0, full - 1, deepen, 0)
            deepen(full - 1, 0)
            state = state_at(full)
            for group in range(groups):
                if group + 1 < groups:
                    push(full, group + 1)
                accumulate(state, group)
            for tile in range(tiles):
                settle(station, tile, pltpu.matmul_pop(sums_of[tile]))
            return carried

        if first:
            for tile in range(tiles):
                settle(stations - 1, tile, None)
            lax.fori_loop(1, stations, one, 0)
        else:
            lax.fori_loop(0, stations, one, 0)

    @pl.when(lax.axis_index("stn") == turn)
    def _():
        pl.run_scoped(
            run, *[pltpu.ACC(tile % UNITS)((PASS_ROWS, TILE), jnp.float32) for tile in range(tiles)]
        )


def march(turn, block, first, incoming, operator, cosine, sine, forcing, slope, sums):
    held = [pltpu.with_memory_space_constraint(v, pltpu.VMEM) for v in (operator, cosine, sine, forcing, slope)]
    return pl.pallas_call(
        functools.partial(march_kernel, turn, block, first),
        out_shape=[jax.ShapeDtypeStruct(v.shape, v.dtype) for v in (sums, incoming)],
        in_specs=[ON_CHIP] * 7,
        out_specs=[ON_CHIP] * 2,
        input_output_aliases={6: 0, 0: 1},
        compiler_params=pltpu.CompilerParams(vmem_limit_bytes=4 << 20),
        name="march",
    )(pltpu.with_memory_space_constraint(incoming, pltpu.VMEM), *held, sums)


def body(propagator, forcing, forward, damping, slowness, station_gap, freq_index):
    stations, _, width = propagator.shape
    freqs = forcing.shape[2]
    chain = lax.axis_size("stn")
    cosine, sine, slope, edge, forcing = prepare(
        station_gap, freq_index, forward, damping[None, :], slowness[None, :], forcing
    )
    rim = from_next(edge, 1)
    half = freqs // BLOCKS
    padded = -(-width // TILE) * TILE
    incoming = [jnp.zeros((2 * half, padded), jnp.bfloat16)] * BLOCKS
    sums = jnp.zeros((stations, width), jnp.float32)
    for turn in range(chain):
        here = chain - 1 - turn
        outgoing = []
        for block in range(BLOCKS):
            sums, out = march(
                here, block, turn == 0, incoming[block],
                propagator, cosine, sine, forcing, slope, sums,
            )
            if here > 0:
                outgoing.append(lax.ppermute(out, "stn", [(here, here - 1)]))
        incoming = outgoing
        if turn == 0:
            slope = finish(station_gap, rim, slope, sums)
            edge, _ = lax.optimization_barrier((edge, sums))
            rim = from_next(edge, 0)
        elif turn == 1:
            slope = finish(station_gap, rim, slope, sums)
    weighting = 1.0 / (4.0 * math.sqrt(freqs * lax.axis_size("freq")))
    return summed_on_arrival(sums * weighting, "freq", 1)


def solution(mesh):
    placed = (
        P("stn", None, None),
        P("stn", None, "freq", None),
        P("stn", None, "freq", None),
        P(),
        P(),
        P("stn"),
        P("freq"),
    )
    with jax.sharding.use_abstract_mesh(mesh.abstract_mesh):
        return jax.shard_map(
            body, mesh=mesh, in_specs=placed, out_specs=P("stn", "freq"), check_vma=False
        )
```
